32 devices in a mesh: row: 8 (over z, x), ba: 4 (over y, core).
Axes of the slice: x: 2, y: 2, z: 4, core: 2. Of those that a mesh axis runs over, the one named last changes fastest.
Arguments:
- constants: float32 [8, 192, 36864], P('row', 'ba'), may hold values from -6 to 6
- current_modes: float32 [8, 2, 192, 4], P('row', None, 'ba'), may hold values from -0.4375 to 0.4375
- owner_id: int32 [1], replicated, may hold values from 0 to 7
- live_count: int32 [8], P('row'), may hold values from 0 to 1, as said below
- triplets: int32 [8, 6], P('row'), may hold values from -3 to 3
- center_point: int32 [3], replicated, may hold values from 0 to 31
- pair_points: int32 [64, 3], P('row'), may hold values from 0 to 31
- first_vectors: float32 [64, 2, 36864], P('row'), may hold values from -0.4375 to 0.4375
- second_vectors: float32 [64, 2, 36864], P('row'), may hold values from -0.4375 to 0.4375
Outputs:
- strength: float32 [64, 4, 36864], P('row', 'ba')
The draws below stay inside these ranges and needn't reach their ends.
Inputs may be any that keep to these rules, and one draw needn't show every extreme that they name: Shard j uses its first live_count[j] slots; the constants and triplets of the other slots are ignored. A shard may use none. Some shard uses all 1 slots.
All inputs are finite; a program needn't handle non-finite values.
Results may differ from the reference program's by a relative error of at most 0.00008.
Values sent between devices are 32-bit elements; how exact they have to be, the bound alone decides.
No kernel may reach another device: no remote copies, remote signals or barrier semaphores. Data moves between devices by JAX's collectives and lax.ppermute only.
A program may use at most 128 MiB of HBM per device.

```python
import math
import jax
import jax.numpy as jnp
from jax import lax

B = 192
BB = 36864
G = 32
R_SLOT = 1
SHARDS = 8
R = 8
QP = 64
NB = 4


def draw_live_count(key, part):
    key_pick = jax.random.fold_in(key, 11)
    key_spread = jax.random.fold_in(key, 12)
    key_full = jax.random.fold_in(key, 13)
    picked = jax.random.randint(key_pick, (SHARDS,), 0, 5)
    spread = jax.random.randint(key_spread, (SHARDS,), 0, R_SLOT + 1)
    counts = jnp.where(picked < 2, 0, spread)
    full_shard = jax.random.randint(key_full, (), 0, SHARDS)
    counts = jnp.where(jnp.arange(SHARDS) == full_shard, R_SLOT, counts)
    return counts.astype(jnp.int32)


def with_ends(values, own_key, low, top_value):
    longest = values.shape.index(max(values.shape))
    spots = []
    for shift in (0, 1):
        where = [jax.random.randint(jax.random.fold_in(own_key, axis), (), 0, length) for axis, length in enumerate(values.shape)]
        where[longest] = (where[longest] + shift) % values.shape[longest]
        spots.append(tuple(where))
    return values.at[spots[0]].set(low).at[spots[1]].set(top_value)


def block_levels(rng, dims, pieces, least, high):
    def one(axis_at, shards_of):
        steps = jax.random.uniform(jax.random.fold_in(jax.random.fold_in(rng, 6), axis_at), (shards_of,), jnp.float32, least / len(pieces), high / len(pieces))
        return jnp.repeat(jnp.exp(steps), dims[axis_at] // shards_of).reshape((-1,) + (1,) * (len(dims) - axis_at - 1))

    level = one(*pieces[0])
    for cut in pieces[1:]:
        level = level * one(*cut)
    return level


def normal_values(own_key, extent, width, most, cuts=(), held_as=jnp.bfloat16):
    values = width * jax.random.normal(own_key, extent, jnp.float32)
    if cuts:
        values = values * block_levels(own_key, extent, cuts, -0.22, 0.18)
    return jnp.clip(values, -most, most).astype(held_as)


def setup_inputs(seed: int = 0) -> dict:
    key_of = jax.random.split(jax.random.key(seed), 10)
    return {
        "constants": normal_values(key_of[0], (R, B, BB), 1.0, 6.0, ((0, 8), (1, 4)), jnp.float32),
        "current_modes": normal_values(key_of[1], (SHARDS, 2, B, NB), B ** -0.5, 0.4375, ((0, 8), (2, 4)), jnp.float32),
        "owner_id": jax.random.randint(key_of[2], (1,), 0, SHARDS).astype(jnp.int32),
        "live_count": draw_live_count(jax.random.fold_in(key_of[9], 71), 0),
        "triplets": with_ends(jax.random.randint(key_of[4], (R, 6), -3, 4), jax.random.fold_in(key_of[4], 1), -3, 3).astype(jnp.int32),
        "center_point": jax.random.randint(key_of[5], (3,), 0, G).astype(jnp.int32),
        "pair_points": with_ends(jax.random.randint(key_of[6], (QP, 3), 0, G), jax.random.fold_in(key_of[6], 1), 0, G - 1).astype(jnp.int32),
        "first_vectors": normal_values(key_of[7], (QP, 2, BB), B ** -0.5, 0.4375, ((0, 8),), jnp.float32),
        "second_vectors": normal_values(key_of[8], (QP, 2, BB), B ** -0.5, 0.4375, ((0, 8),), jnp.float32),
    }


HIGHEST = lax.Precision.HIGHEST
FULL_TURN = 2.0 * math.pi


def rotation_table(pair_rows, shift_rows, grid_size):
    turns = jnp.sum(pair_rows[:, :, None] * shift_rows[None, 0:3, :], axis=1) - shift_rows[3][None, :]
    angle = jnp.mod(turns, grid_size).astype(jnp.float32) * (FULL_TURN / grid_size)
    cosine = jnp.cos(angle)
    sine = jnp.sin(angle)
    upper_row = jnp.stack([cosine, -sine], axis=1)
    lower_row = jnp.stack([sine, cosine], axis=1)
    return jnp.stack([upper_row, lower_row], axis=1)


def complex_block(vectors, branches):
    pair_count = vectors.shape[0]
    real_part = vectors[:, 0].reshape(pair_count, branches, branches)
    imag_part = vectors[:, 1].reshape(pair_count, branches, branches)
    upper_row = jnp.stack([real_part, -imag_part], axis=1)
    lower_row = jnp.stack([imag_part, real_part], axis=1)
    return jnp.stack([upper_row, lower_row], axis=1)


def strengths(phase_sum, first_vectors, second_vectors, branches, total_slots):
    pair_count = phase_sum.shape[0]
    band_count = phase_sum.shape[1]
    shaped = phase_sum.reshape(pair_count, band_count, 2, branches, branches)
    partial_sum = jnp.einsum("knibc,koicm->knobm", shaped, complex_block(second_vectors, branches), precision=HIGHEST)
    amplitude = jnp.einsum("kojbp,knjbm->knopm", complex_block(first_vectors, branches), partial_sum, precision=HIGHEST)
    result = (amplitude[:, :, 0] * amplitude[:, :, 0] + amplitude[:, :, 1] * amplitude[:, :, 1]) / total_slots
    return result.reshape(pair_count, band_count, branches * branches)


def reference(constants, current_modes, owner_id, live_count, triplets, center_point, pair_points, first_vectors, second_vectors):
    eigen = current_modes[owner_id[0]]
    slot_index = jnp.arange(R, dtype=jnp.int32)
    weight = ((slot_index % R_SLOT) < live_count[slot_index // R_SLOT]).astype(jnp.float32)
    contracted = jnp.einsum("san,rax->nsrx", eigen, constants, precision=HIGHEST)
    contracted = contracted * weight[None, None, :, None]
    second_cell = triplets[:, 3:6]
    offsets = triplets[:, 0:3] - second_cell
    point_shift = jnp.sum(second_cell * center_point[None, :], axis=1)
    shift_rows = jnp.concatenate([offsets.T, point_shift[None, :]], axis=0)
    rotation = rotation_table(pair_points, shift_rows, G)
    phase_sum = jnp.einsum("kuir,nirx->knux", rotation, contracted, precision=HIGHEST)
    return strengths(phase_sum, first_vectors, second_vectors, B, R)
```

```python
import functools
import math

import jax
import jax.numpy as jnp
import numpy as np
from jax import lax
from jax.experimental import pallas as pl
from jax.experimental.pallas import tpu as pltpu
from jax.sharding import PartitionSpec as P

G = 32
FULL_TURN = 2.0 * math.pi
LANES = 128
F32 = jnp.float32
BF16 = jnp.bfloat16
VMEM = pltpu.VMEM
SMEM = pltpu.SMEM


def split(x):
    hi = x.astype(BF16)
    lo = (x - hi.astype(F32)).astype(BF16)
    return hi, lo


def dot(a, b):
    return jnp.dot(a, b, preferred_element_type=F32)


def pack_kernel(bands, slots, ids, owner, trip, center, modes, out):
    row, ba = ids[0], ids[1]
    out[...] = jnp.zeros_like(out)
    mine = (owner[0] == row).astype(F32)
    width = modes.shape[-1]
    order = [j for j in range(bands) if j % 2 == 0] + [j for j in range(bands) if j % 2]
    for place, j in enumerate(order):
        for s in range(2):
            line = modes[s, pl.ds(lax.bitwise_xor(ba, j), 1), :]
            out[pl.ds(place * 2 + s, 1), 0:width] = line * mine
    lane = lax.broadcasted_iota(jnp.int32, (1, LANES), 1)
    for r in range(slots):
        entry = jnp.zeros((1, LANES), jnp.int32)
        shift = 0
        for d in range(3):
            entry = jnp.where(lane == d, trip[r, d] - trip[r, 3 + d], entry)
            shift = shift + trip[r, 3 + d] * center[d]
        entry = jnp.where(lane == 3, shift, entry)
        out[pl.ds(2 * bands + row * slots + r, 1), :] = entry.astype(F32)


def pack(modes, owner, trip, center, ids, bands, slots, total):
    rows = 2 * bands + -(-total // 8) * 8
    return pl.pallas_call(
        functools.partial(pack_kernel, bands, slots),
        out_shape=jax.ShapeDtypeStruct((rows, LANES), F32),
        in_specs=[pl.BlockSpec(memory_space=SMEM)] * 4 + [pl.BlockSpec(memory_space=VMEM)],
        out_specs=pl.BlockSpec(memory_space=VMEM),
        name="pack",
    )(ids, owner, trip, center, modes)


def contract_kernel(bands, slots, lines, live, e0, e1, const, keep, send):
    width = const.shape[1]
    total = e0[...] + e1[...]
    eigen = total[0 : 2 * bands, 0:width]
    chunk = 3 * LANES
    for r in range(slots):
        weight = (r < live[0]).astype(F32)
        eh, el = split(eigen * weight)
        ch, cl = split(const[r])
        both = dot(jnp.concatenate([eh, el], axis=0), ch)
        res = both[0 : 2 * bands] + both[2 * bands :] + dot(eh, cl)
        for q in range(lines):
            part = res[:, q * chunk : (q + 1) * chunk]
            keep[:, r, q, :] = part[0:bands]
            send[:, r, q, :] = part[bands:]


def contract(constants, e0, e1, live, bands):
    slots, width, bb = constants.shape
    chunk = 3 * LANES
    pairs = bb // chunk
    lines = 8
    out = jax.ShapeDtypeStruct((bands, slots, pairs, chunk), F32)
    whole = pl.BlockSpec(e0.shape, lambda i: (0, 0))
    return pl.pallas_call(
        functools.partial(contract_kernel, bands, slots, lines),
        out_shape=(out, out),
        grid=(pairs // lines,),
        in_specs=[
            pl.BlockSpec(memory_space=SMEM),
            whole,
            whole,
            pl.BlockSpec((slots, width, lines * chunk), lambda i: (0, 0, i)),
        ],
        out_specs=[pl.BlockSpec((bands, slots, lines, chunk), lambda i: (0, 0, i, 0))] * 2,
        name="contract",
    )(live, e0, e1, constants)


def unpack_matrix(ref, s, size):
    half = size // 2
    step = 6
    j0, j1, j2 = (ref[0, pl.ds(2 * j + s, half, stride=step), :] for j in range(3))
    lane = lax.broadcasted_iota(jnp.int32, j0.shape, 1)
    r1 = pltpu.roll(j1, 64, 1)
    r2 = pltpu.roll(j2, 64, 1)
    return (j0, j1), (jnp.where(lane < 64, r1, r2), r2)


def join(a, b, size):
    return jnp.concatenate([a, b[:, 0 : size - LANES]], axis=1)


def prep_kernel(size, first, second, gh, gl, wh, wl, lo, hi):
    half = size // 2
    mats = []
    for s in range(2):
        even, odd = unpack_matrix(first, s, size)
        turned = jnp.concatenate([join(*even, size), join(*odd, size)], axis=0).T
        lo[...] = turned[:, 0:LANES]
        hi[:, 0 : size - LANES] = turned[:, LANES:size]
        rows = [
            join(lo[pl.ds(p, half, stride=2), :], hi[pl.ds(p, half, stride=2), :], size)
            for p in range(2)
        ]
        mats.append(jnp.concatenate(rows, axis=0))
    for i, m in enumerate((mats[0] + mats[1], mats[0], mats[1])):
        gh[0, i], gl[0, i] = split(m)
    mats = []
    for s in range(2):
        for p, (a, b) in enumerate(unpack_matrix(second, s, size)):
            lo[pl.ds(p, half, stride=2), :] = a
            hi[pl.ds(p, half, stride=2), :] = b
        mats.append(join(lo[...], hi[...], size))
    for i, m in enumerate((mats[0], mats[1] - mats[0], mats[0] + mats[1])):
        wh[0, i], wl[0, i] = split(m)


def prep(first, second, size):
    count, _, bb = first.shape
    tiles = bb // LANES

    def view(a):
        return a.reshape(count, 2, tiles, LANES).swapaxes(1, 2).reshape(count, 2 * tiles, LANES)

    out = jax.ShapeDtypeStruct((count, 3, size, size), BF16)
    return pl.pallas_call(
        functools.partial(prep_kernel, size),
        out_shape=(out,) * 4,
        grid=(count,),
        in_specs=[pl.BlockSpec((1, 2 * tiles, LANES), lambda k: (k, 0, 0))] * 2,
        out_specs=[pl.BlockSpec((1, 3, size, size), lambda k: (k, 0, 0, 0))] * 4,
        scratch_shapes=[VMEM((size, LANES), F32)] * 2,
        name="prep",
    )(view(first), view(second))


def final_kernel(spec, scale, size, *refs):
    blocks = refs[: len(spec)]
    cs, gh, gl, wh, wl, out, ph, plo, ares = refs[len(spec) :]
    half = size // 2
    k = pl.program_id(0)
    group = 16
    for g in range(half // group):
        q0 = g * group
        re = im = None
        for ref, (base, lines, slots) in zip(blocks, spec):
            if not base <= q0 < base + lines:
                continue
            local = pl.ds(q0 - base, group)
            if len(slots) <= 8:
                for t, slot in enumerate(slots):
                    c, s = cs[k, 2 * slot], cs[k, 2 * slot + 1]
                    a, b = ref[t, 0, local, :], ref[t, 1, local, :]
                    r_new, i_new = a * c - b * s, a * s + b * c
                    re = r_new if re is None else re + r_new
                    im = i_new if im is None else im + i_new
            else:
                zero = jnp.zeros((group, 3 * LANES), F32)

                def step(t, carry):
                    c, s = cs[k, 2 * t], cs[k, 2 * t + 1]
                    a, b = ref[t, 0, local, :], ref[t, 1, local, :]
                    return carry[0] + (a * c - b * s), carry[1] + (a * s + b * c)

                re, im = lax.fori_loop(0, len(slots), step, (zero, zero))
        for i, m in enumerate((re + im, re, im)):
            hi, lo = split(m)
            for base, lanes in ((0, slice(0, size)), (half, slice(size, 2 * size))):
                ph[i, pl.ds(base + q0, group), :] = hi[:, lanes]
                plo[i, pl.ds(base + q0, group), :] = lo[:, lanes]

    def triple(xh, xl, yh, yl):
        return dot(xh, yh) + dot(xl, yh) + dot(xh, yl)

    k1, k2, k3 = (triple(ph[i], plo[i], wh[0, i], wl[0, i]) for i in range(3))
    tr, ti = k1 - k3, k1 + k2
    terms = []
    for i, m in enumerate((tr, ti - tr, tr + ti)):
        mh, ml = split(m)
        terms.append(triple(gh[0, i], gl[0, i], mh, ml))
    ar, ai = terms[0] - terms[2], terms[0] + terms[1]
    ares[:, 0:size] = (ar * ar + ai * ai) * scale
    e0, e1 = ares[0:half, 0:LANES], ares[0:half, LANES : 2 * LANES]
    o0, o1 = ares[half:size, 0:LANES], ares[half:size, LANES : 2 * LANES]
    low = lax.broadcasted_iota(jnp.int32, e0.shape, 1) < 64
    r0, r1 = pltpu.roll(o0, 64, 1), pltpu.roll(o1, 64, 1)
    out[0, pl.ds(0, half, stride=3), :] = e0
    out[0, pl.ds(1, half, stride=3), :] = jnp.where(low, e1, r0)
    out[0, pl.ds(2, half, stride=3), :] = jnp.where(low, r0, r1)


def final(blocks, spec, cs, operands, total):
    count, _, size, _ = operands[0].shape
    tiles = size * size // LANES
    mats = [pl.BlockSpec((1, 3, size, size), lambda k: (k, 0, 0, 0))] * 4
    result = pl.pallas_call(
        functools.partial(final_kernel, spec, 1.0 / total, size),
        out_shape=jax.ShapeDtypeStruct((count, tiles, LANES), F32),
        grid=(count,),
        in_specs=[pl.BlockSpec(memory_space=VMEM)] * len(blocks)
        + [pl.BlockSpec(memory_space=SMEM)]
        + mats,
        out_specs=pl.BlockSpec((1, tiles, LANES), lambda k: (k, 0, 0)),
        scratch_shapes=[
            VMEM((3, size, size), BF16),
            VMEM((3, size, size), BF16),
            VMEM((size, 2 * LANES), F32),
        ],
        name="final",
    )(*blocks, cs, *operands)
    return result.reshape(count, 1, size * size)


def swap(x, axis, bit, n):
    return lax.ppermute(x, axis, [(i, i ^ bit) for i in range(n)])


def edges(n):
    cycle = list(range(0, n, 2)) + list(range(n - 1, 0, -2))
    even, odd = [], []
    for i in range(0, n, 2):
        a, b, c = cycle[i], cycle[i + 1], cycle[(i + 2) % n]
        even += [(a, b), (b, a)]
        odd += [(b, c), (c, b)]
    return even, odd


def neighbour_gather(parts, n):
    even, odd = edges(n)
    plans = ((even, odd), (odd, even))
    blocks, sources = [[p[None]] for p in parts], [[np.arange(n)[:, None]] for _ in parts]
    moving = [b[0] for b in blocks]
    held = [s[0] for s in sources]
    for step in range(n // 2):
        arrived = []
        for h, plan in enumerate(plans):
            perm = plan[step % 2]
            arrived.append(lax.ppermute(moving[h], "row", perm))
            source = np.zeros_like(held[h])
            for a, b in perm:
                source[b] = held[h][a]
            blocks[h].append(arrived[h])
            sources[h].append(source)
            if step == 0:
                held[h] = np.concatenate([held[h], source], axis=1)
            else:
                held[h] = source
        for h in range(2):
            moving[h] = (
                jnp.concatenate([moving[h], arrived[h]]) if step == 0 else arrived[h]
            )
    return blocks, [np.concatenate(s, axis=1) for s in sources]


def body(
    constants,
    current_modes,
    owner_id,
    live_count,
    triplets,
    center_point,
    pair_points,
    first_vectors,
    second_vectors,
):
    n_row, n_ba = lax.axis_size("row"), lax.axis_size("ba")
    slots, width, bb = constants.shape
    size = width * n_ba
    bands = current_modes.shape[-1]
    half = size // 2
    total = slots * n_row
    row, ba = lax.axis_index("row"), lax.axis_index("ba")
    ids = jnp.stack([row, ba]).astype(jnp.int32)

    modes = jnp.swapaxes(current_modes[0], 1, 2)
    payload = pack(modes, owner_id, triplets, center_point, ids, bands, slots, total)
    bit = 1
    while bit < n_row:
        other = swap(payload, "row", bit, n_row)
        bit *= 2
        if bit < n_row:
            payload = payload + other
    keep, send = contract(constants, payload, other, live_count, bands)
    geometry = (payload + other)[2 * bands : 2 * bands + total, 0:4].astype(jnp.int32)

    keep = keep.reshape(bands // 2, 2, slots, half, 2 * size)
    send = send.reshape(bands // 2, 2, slots, half, 2 * size)
    got = swap(send, "ba", 1, n_ba)
    far = swap(keep[1] + got[1], "ba", 2, n_ba)
    own = (keep[0] + got[0]) + far
    own = own.swapaxes(0, 1)

    turns = (
        jnp.sum(pair_points[:, :, None] * geometry.T[None, 0:3, :], axis=1)
        - geometry[:, 3][None, :]
    )
    angle = jnp.mod(turns, G).astype(F32) * (FULL_TURN / G)
    table = jnp.stack([jnp.cos(angle), jnp.sin(angle)], axis=-1)

    operands = prep(first_vectors, second_vectors, size)
    if slots == 1 and n_row <= 8:
        parts = (own[0, :, : half // 2], own[0, :, half // 2 :])
        blocks, sources = neighbour_gather(parts, n_row)
        order = jnp.asarray(np.concatenate(sources, axis=1))[row]
        table = table[:, order].reshape(table.shape[0], -1)
        arrays, spec = [], []
        for h in range(2):
            slot = h * n_row
            for b in blocks[h]:
                arrays.append(b)
                spec.append((h * half // 2, half // 2, tuple(range(slot, slot + b.shape[0]))))
                slot += b.shape[0]
    else:
        arrays = [lax.all_gather(own, "row", axis=0, tiled=True)]
        spec = [(0, half, tuple(range(total)))]
        table = table.reshape(table.shape[0], -1)
    return final(arrays, tuple(spec), table, operands, total)


def solution(mesh):
    return jax.shard_map(
        body,
        mesh=mesh,
        in_specs=(
            P("row", "ba", None),
            P("row", None, "ba", None),
            P(),
            P("row"),
            P("row", None),
            P(),
            P("row", None),
            P("row", None, None),
            P("row", None, None),
        ),
        out_specs=P("row", "ba", None),
        check_vma=False,
    )
```

```python
import functools
import math

import jax
import jax.numpy as jnp
import numpy as np
from jax import lax
from jax.experimental import pallas as pl
from jax.experimental.pallas import tpu as pltpu
from jax.sharding import PartitionSpec as P

G = 32
FULL_TURN = 2.0 * math.pi
LANES = 128
F32 = jnp.float32
BF16 = jnp.bfloat16
VMEM = pltpu.VMEM
SMEM = pltpu.SMEM


def split(x):
    hi = x.astype(BF16)
    lo = (x - hi.astype(F32)).astype(BF16)
    return hi, lo


def dot(a, b):
    return jnp.dot(a, b, preferred_element_type=F32)


def in_vmem(*xs):
    return [pltpu.with_memory_space_constraint(x, VMEM) for x in xs]


def kept(shape, dtype=F32):
    return VMEM(shape, dtype)


WHOLE = pl.BlockSpec(memory_space=VMEM)
SCALARS = pl.BlockSpec(memory_space=SMEM)
RAW = pl.BlockSpec(memory_space=pltpu.HBM)


def limit(mib):
    return pltpu.CompilerParams(vmem_limit_bytes=mib << 20)


def pack_kernel(bands, slots, *refs):
    raw, out, (owner, trip, center, live, modes, sem) = refs[:5], refs[5], refs[6:]
    copies = [
        pltpu.make_async_copy(src, dst, sem.at[i])
        for i, (src, dst) in enumerate(zip(raw, (owner, trip, center, live, modes)))
    ]
    for c in copies:
        c.start()
    out[...] = jnp.zeros_like(out)
    for c in copies:
        c.wait()
    row, ba = lax.axis_index("row"), lax.axis_index("ba")
    mine = (owner[0] == row).astype(F32)
    width = modes.shape[-1]
    order = [j for j in range(bands) if j % 2 == 0] + [j for j in range(bands) if j % 2]
    for place, j in enumerate(order):
        for s in range(2):
            line = modes[s, pl.ds(lax.bitwise_xor(ba, j), 1), :]
            out[pl.ds(place * 2 + s, 1), 0:width] = line * mine
    lane = lax.broadcasted_iota(jnp.int32, (1, LANES), 1)
    for r in range(slots):
        shift = 0
        entry = jnp.where(lane == 4, (r < live[0]).astype(jnp.int32), 0)
        for d in range(3):
            entry = jnp.where(lane == d, trip[r, d] - trip[r, 3 + d], entry)
            shift = shift + trip[r, 3 + d] * center[d]
        entry = jnp.where(lane == 3, shift, entry)
        out[pl.ds(2 * bands + row * slots + r, 1), :] = entry.astype(F32)


def pack(modes, owner, trip, center, live, bands, slots, total):
    rows = 2 * bands + -(-total // 8) * 8
    ints = (owner, trip, center, live)
    return pl.pallas_call(
        functools.partial(pack_kernel, bands, slots),
        out_shape=kept((rows, LANES)),
        in_specs=[RAW] * 5,
        out_specs=WHOLE,
        scratch_shapes=[SMEM(x.shape, x.dtype) for x in ints]
        + [VMEM(modes.shape, F32), pltpu.SemaphoreType.DMA((5,))],
        compiler_params=limit(4),
        name="pack",
    )(*ints, modes)


def fetch_kernel(slots, first, rows, parts, const, hi, lo, buf, sem):
    width = const.shape[2] // parts
    copies = []
    for r in range(slots):
        for i in range(parts):
            lanes = pl.ds(i * width, width)
            copies.append(
                pltpu.make_async_copy(
                    const.at[r, pl.ds(first, rows), lanes], buf.at[r, :, lanes], sem.at[r, i]
                )
            )
    for c in copies:
        c.start()
    for n, c in enumerate(copies):
        c.wait()
        r, i = n // parts, n % parts
        lanes = slice(i * width, (i + 1) * width)
        hi[r, :, lanes], lo[r, :, lanes] = split(buf[r, :, lanes])


def fetch(constants, first, rows):
    slots, _, bb = constants.shape
    parts = 6
    return pl.pallas_call(
        functools.partial(fetch_kernel, slots, first, rows, parts),
        out_shape=(kept((slots, rows, bb), BF16),) * 2,
        in_specs=[RAW],
        out_specs=[WHOLE] * 2,
        scratch_shapes=[
            VMEM((slots, rows, bb), F32),
            pltpu.SemaphoreType.DMA((slots, parts)),
        ],
        compiler_params=limit(8),
        name="fetch",
    )(constants)


def contract_kernel(bands, slots, lines, e0, e1, *refs):
    pieces, (keep, send) = refs[:-2], refs[-2:]
    his, los = pieces[0::2], pieces[1::2]
    width = sum(h.shape[1] for h in his)
    total = e0[...] + e1[...]
    eigen = total[0 : 2 * bands, 0:width]
    pairs, chunk = keep.shape[2], keep.shape[3]
    low = lax.broadcasted_iota(jnp.int32, (2 * bands, LANES), 1) < 64
    for r in range(slots):
        own = pl.ds(2 * bands + lax.axis_index("row") * slots + r, 1)
        weight = e0[own, 4:5] + e1[own, 4:5]
        eh, el = split(eigen * weight)
        left = jnp.concatenate(
            [
                jnp.concatenate([eh, eh], axis=1),
                jnp.concatenate([el, jnp.zeros_like(el)], axis=1),
            ],
            axis=0,
        )
        for base in range(0, pairs, lines):
            lanes = slice(base * chunk, (base + lines) * chunk)
            right = jnp.concatenate(
                [h[r, :, lanes] for h in his] + [m[r, :, lanes] for m in los], axis=0
            )
            both = dot(left, right)
            res = both[0 : 2 * bands] + both[2 * bands :]
            for q in range(lines):
                j0, j1, j2 = (
                    res[:, q * chunk + j * LANES : q * chunk + (j + 1) * LANES]
                    for j in range(3)
                )
                t1 = jnp.where(low, j1, j2)
                t2 = jnp.where(low, pltpu.roll(j1, 64, 1), pltpu.roll(j2, 64, 1))
                for j, t in enumerate((j0, t1, t2)):
                    spot = slice(j * LANES, (j + 1) * LANES)
                    keep[:, r, base + q, spot] = t[0:bands]
                    send[:, r, base + q, spot] = t[bands:]


def contract(pieces, e0, e1, bands):
    slots, _, bb = pieces[0].shape
    chunk = 3 * LANES
    return pl.pallas_call(
        functools.partial(contract_kernel, bands, slots, 8),
        out_shape=(kept((bands, slots, bb // chunk, chunk)),) * 2,
        in_specs=[WHOLE] * (2 + len(pieces)),
        out_specs=[WHOLE] * 2,
        compiler_params=limit(8),
        name="contract",
    )(*in_vmem(e0, e1, *pieces))


def unpack_matrix(ref, k, s, size):
    half = size // 2
    j0, j1, j2 = (ref[k, pl.ds(2 * j + s, half, stride=6), :] for j in range(3))
    lane = lax.broadcasted_iota(jnp.int32, j0.shape, 1)
    r1 = pltpu.roll(j1, 64, 1)
    r2 = pltpu.roll(j2, 64, 1)
    return (j0, j1), (jnp.where(lane < 64, r1, r2), r2)


def join(a, b, size):
    return jnp.concatenate([a, b[:, 0 : size - LANES]], axis=1)


def prep_kernel(size, turn, raw, hi, lo, buf, sem, left, right):
    half = size // 2
    count = raw.shape[0]
    copies = [
        pltpu.make_async_copy(raw.at[k], buf.at[k], sem.at[k]) for k in range(count)
    ]
    for c in copies:
        c.start()
    for k in range(count):
        copies[k].wait()
        mats = []
        for s in range(2):
            even, odd = unpack_matrix(buf, k, s, size)
            if turn:
                turned = jnp.concatenate([join(*even, size), join(*odd, size)], axis=0).T
                left[...] = turned[:, 0:LANES]
                right[:, 0 : size - LANES] = turned[:, LANES:size]
                rows = [
                    join(
                        left[pl.ds(p, half, stride=2), :],
                        right[pl.ds(p, half, stride=2), :],
                        size,
                    )
                    for p in range(2)
                ]
                mats.append(jnp.concatenate(rows, axis=0))
            else:
                for p, (a, b) in enumerate((even, odd)):
                    left[pl.ds(p, half, stride=2), :] = a
                    right[pl.ds(p, half, stride=2), :] = b
                mats.append(join(left[...], right[...], size))
        re, im = mats
        three = (re + im, re, im) if turn else (re, im - re, re + im)
        for i, m in enumerate(three):
            hi[k, i], lo[k, i] = split(m)


def prep(vectors, size, turn):
    count, _, bb = vectors.shape
    tiles = bb // LANES
    view = vectors.reshape(count, 2, tiles, LANES).swapaxes(1, 2)
    view = view.reshape(count, 2 * tiles, LANES)
    return pl.pallas_call(
        functools.partial(prep_kernel, size, turn),
        out_shape=(kept((count, 3, size, size), BF16),) * 2,
        in_specs=[RAW],
        out_specs=[WHOLE] * 2,
        scratch_shapes=[
            VMEM(view.shape, F32),
            pltpu.SemaphoreType.DMA((count,)),
            VMEM((size, LANES), F32),
            VMEM((size, LANES), F32),
        ],
        compiler_params=limit(8),
        name="prep",
    )(view)


def angle_kernel(first, order, e0, e1, points, out):
    count, width = points.shape[1], len(order[0])
    row = lax.axis_index("row")
    lines = []
    for choice in zip(*order):
        if len(set(choice)) == 1:
            slot = choice[0]
        else:
            slot = sum(jnp.where(row == i, c, 0) for i, c in enumerate(choice))
        spot = pl.ds(first + slot, 1)
        lines.append(e0[spot, :] + e1[spot, :])
    lines = jnp.concatenate(lines, axis=0)
    cell = [jnp.broadcast_to(lines[:, d : d + 1], (width, LANES)) for d in range(4)]
    for k in range(count):
        turns = -cell[3]
        for d in range(3):
            turns = turns + cell[d] * points[d : d + 1, k : k + 1].astype(F32)
        turns = lax.rem(turns.astype(jnp.int32), G)
        turns = jnp.where(turns < 0, turns + G, turns)
        angle = turns.astype(F32) * (FULL_TURN / G)
        out[0, k * width : (k + 1) * width, :] = jnp.cos(angle)
        out[1, k * width : (k + 1) * width, :] = jnp.sin(angle)


def angles(e0, e1, points, first, order):
    lines = points.shape[0] * len(order[0])
    return pl.pallas_call(
        functools.partial(angle_kernel, first, order),
        out_shape=kept((2, lines, LANES)),
        in_specs=[WHOLE] * 3,
        out_specs=WHOLE,
        compiler_params=limit(4),
        name="angles",
    )(*in_vmem(e0, e1), points.T)


def rotated(refs, spec, cs, width, k, q0, group, re, im):
    for ref, (base, lines, slots) in zip(refs, spec):
        if not base <= q0 < base + lines:
            continue
        local = pl.ds(q0 - base, group)

        def turn(t, slot):
            spot = pl.ds(k * width + slot, 1)
            c, s = cs[0, spot, :], cs[1, spot, :]
            a, b = ref[t, 0, local, :], ref[t, 1, local, :]
            c, s = (jnp.concatenate([x] * 3, axis=1) for x in (c, s))
            return a * c - b * s, a * s + b * c

        if len(slots) <= 8:
            for t, slot in enumerate(slots):
                a, b = turn(t, slot)
                re = a if re is None else re + a
                im = b if im is None else im + b
        else:
            zero = jnp.zeros((group, 3 * LANES), F32)

            def step(t, carry):
                a, b = turn(t, t)
                return carry[0] + a, carry[1] + b

            start = (zero if re is None else re, zero if im is None else im)
            re, im = lax.fori_loop(0, len(slots), step, start)
    return re, im


def early_kernel(spec, width, group, *refs):
    blocks, cs, out = refs[: len(spec)], refs[-2], refs[-1]

    def one(k, carry):
        for q0 in range(0, out.shape[2], group):
            re, im = rotated(blocks, spec, cs, width, k, q0, group, None, None)
            out[k, 0, pl.ds(q0, group), :] = re
            out[k, 1, pl.ds(q0, group), :] = im
        return carry

    lax.fori_loop(0, out.shape[0], one, 0)


def early(blocks, spec, cs, count, half):
    width = cs.shape[1] // count
    return pl.pallas_call(
        functools.partial(early_kernel, spec, width, 8),
        out_shape=kept((count, 2, half, 3 * LANES)),
        in_specs=[WHOLE] * (len(blocks) + 1),
        out_specs=WHOLE,
        compiler_params=limit(4),
        name="early",
    )(*in_vmem(*blocks, cs))


def final_kernel(spec, width, scale, size, unroll, partial, *refs):
    blocks = refs[: len(spec)]
    cs, gh, gl, wh, wl, out, ph, plo = refs[len(spec) :]
    half = size // 2
    group = 16
    first = pl.program_id(0) * unroll

    def load(u):
        k = first + u
        for q0 in range(0, half, group):
            re, im = partial[k, 0, pl.ds(q0, group), :], partial[k, 1, pl.ds(q0, group), :]
            re, im = rotated(blocks, spec, cs, width, k, q0, group, re, im)
            for i, m in enumerate((re + im, re, im)):
                t0, t1, t2 = (m[:, j * LANES : (j + 1) * LANES] for j in range(3))
                for base, a, b in ((0, t0, t1), (half, t2, pltpu.roll(t1, 64, 1))):
                    spot = pl.ds(base + q0, group)
                    for dst, x, y in zip((ph, plo), split(a), split(b)):
                        dst[u, i, spot, 0:LANES] = x
                        dst[u, i, spot, LANES : 2 * LANES] = y

    def triple(xh, xl, yh, yl):
        both = dot(jnp.concatenate([xh, xl], axis=0), yh)
        return both[0:size] + both[size:] + dot(xh, yl)

    def inner(u):
        k = first + u
        k1, k2, k3 = (
            triple(ph[u, i][:, 0:size], plo[u, i][:, 0:size], wh[k, i], wl[k, i])
            for i in range(3)
        )
        return k1 - k3, k1 + k2

    def outer(u, re, im):
        k = first + u
        k1, k2, k3 = (
            triple(gh[k, i], gl[k, i], *split(m))
            for i, m in enumerate((re, im - re, re + im))
        )
        re, im = k1 - k3, k1 + k2
        return (re * re + im * im) * scale

    def store(u, value):
        tail = value[:, LANES:size]
        tail = jnp.concatenate([tail, tail], axis=1)
        turned = pltpu.roll(value[half:, 0:LANES], 64, 1)
        low = lax.broadcasted_iota(jnp.int32, turned.shape, 1) < 64
        out[u, pl.ds(0, half, stride=3), :] = value[0:half, 0:LANES]
        out[u, pl.ds(1, half, stride=3), :] = jnp.where(low, tail[0:half], turned)
        out[u, pl.ds(2, half, stride=3), :] = jnp.where(low, turned, tail[half:])

    for u in range(unroll):
        load(u)
    sums = [inner(u) for u in range(unroll)]
    for u in range(unroll):
        store(u, outer(u, *sums[u]))


def final(partial, blocks, spec, cs, operands, total):
    count, _, size, _ = operands[0].shape
    tiles = size * size // LANES
    unroll = 2 if count % 2 == 0 else 1
    result = pl.pallas_call(
        functools.partial(final_kernel, spec, cs.shape[1] // count, 1.0 / total, size, unroll),
        out_shape=jax.ShapeDtypeStruct((count, tiles, LANES), F32),
        grid=(count // unroll,),
        in_specs=[WHOLE] * (6 + len(blocks)),
        out_specs=pl.BlockSpec((unroll, tiles, LANES), lambda k: (k, 0, 0)),
        scratch_shapes=[VMEM((unroll, 3, size, 2 * LANES), BF16)] * 2,
        compiler_params=limit(16),
        name="final",
    )(*in_vmem(partial, *blocks, cs, *operands))
    return result.reshape(count, 1, size * size)


def swap(x, axis, bit, n):
    return lax.ppermute(x, axis, [(i, i ^ bit) for i in range(n)])


def edges(n):
    cycle = list(range(0, n, 2)) + list(range(n - 1, 0, -2))
    even, odd = [], []
    for i in range(0, n, 2):
        a, b, c = cycle[i], cycle[i + 1], cycle[(i + 2) % n]
        even += [(a, b), (b, a)]
        odd += [(b, c), (c, b)]
    return even, odd


def neighbour_gather(parts, n):
    even, odd = edges(n)
    plans = ((even, odd), (odd, even))
    moving = [p[None] for p in parts]
    held = [np.arange(n)[:, None] for _ in parts]
    blocks, sources = [[], []], [[], []]
    for step in range(n // 2):
        arrived = []
        for h, plan in enumerate(plans):
            perm = plan[step % 2]
            with jax.named_scope(f"ring{step}{'ab'[h]}"):
                arrived.append(lax.ppermute(moving[h], "row", perm))
            source = np.zeros_like(held[h])
            for a, b in perm:
                source[b] = held[h][a]
            if step == 0:
                source = np.concatenate([held[h], source], axis=1)
            held[h] = source
            sources[h].append(source)
        for h in range(2):
            if step == 0:
                arrived[h] = jnp.concatenate([moving[h], arrived[h]])
            moving[h] = arrived[h]
            blocks[h].append(moving[h])
    return blocks, [np.concatenate(s, axis=1) for s in sources]


def body(
    constants,
    current_modes,
    owner_id,
    live_count,
    triplets,
    center_point,
    pair_points,
    first_vectors,
    second_vectors,
):
    n_row, n_ba = lax.axis_size("row"), lax.axis_size("ba")
    slots, width, bb = constants.shape
    size = width * n_ba
    bands = current_modes.shape[-1]
    half = size // 2
    total = slots * n_row
    scope = jax.named_scope
    modes = jnp.swapaxes(current_modes[0], 1, 2)
    payload = pack(
        modes, owner_id, triplets, center_point, live_count, bands, slots, total
    )
    bit, hop = 1, 0
    while bit < n_row:
        with scope(f"hop{hop}"):
            other = swap(payload, "row", bit, n_row)
        bit, hop = bit * 2, hop + 1
        if bit < n_row:
            payload = payload + other
    cuts = 3 if width % 48 == 0 else 1
    pieces = []
    for i in range(cuts):
        with scope(f"fetch{i}"):
            pieces += fetch(constants, i * width // cuts, width // cuts)
    keep, send = contract(pieces, payload, other, bands)

    keep = keep.reshape(bands // 2, 2, slots, half, 2 * size)
    send = send.reshape(bands // 2, 2, slots, half, 2 * size)
    with scope("core"):
        got = swap(send, "ba", 1, n_ba)
    with scope("far"):
        far = swap(keep[1] + got[1], "ba", 2, n_ba)
    own = (keep[0] + got[0]) + far
    own = own.swapaxes(0, 1)

    with scope("weights"):
        weights = prep(second_vectors, size, False)
    with scope("lefts"):
        lefts = prep(first_vectors, size, True)
    operands = (*lefts, *weights)
    if slots == 1 and n_row <= 8:
        parts = (own[0, :, : half // 2], own[0, :, half // 2 :])
        blocks, sources = neighbour_gather(parts, n_row)
        order = np.concatenate(sources, axis=1)
        ahead, behind = [], []
        for h in range(2):
            slot = h * n_row
            for n, b in enumerate(blocks[h]):
                here = range(slot, slot + b.shape[0])
                entry = (b, (h * half // 2, half // 2, tuple(here)))
                (behind if n == len(blocks[h]) - 1 else ahead).append(entry)
                slot += b.shape[0]
    else:
        gathered = lax.all_gather(own, "row", axis=0, tiled=True)
        ahead, behind = [(gathered, (0, half, tuple(range(total))))], []
        order = np.broadcast_to(np.arange(total), (n_row, total))
    order = tuple(tuple(int(x) for x in line) for line in order)
    with scope("angles"):
        table = angles(payload, other, pair_points, 2 * bands, order)
    arrays, spec = zip(*ahead)
    with scope("early"):
        partial = early(arrays, spec, table, pair_points.shape[0], half)
    arrays, spec = zip(*behind) if behind else ((), ())
    return final(partial, arrays, spec, table, operands, total)


def solution(mesh):
    return jax.shard_map(
        body,
        mesh=mesh,
        in_specs=(
            P("row", "ba", None),
            P("row", None, "ba", None),
            P(),
            P("row"),
            P("row", None),
            P(),
            P("row", None),
            P("row", None, None),
            P("row", None, None),
        ),
        out_specs=P("row", "ba", None),
        check_vma=False,
    )
```

```python
import functools
import math

import jax
import jax.numpy as jnp
import numpy as np
from jax import lax
from jax.experimental import pallas as pl
from jax.experimental.pallas import tpu as pltpu
from jax.sharding import PartitionSpec as P

G = 32
FULL_TURN = 2.0 * math.pi
LANES = 128
F32 = jnp.float32
BF16 = jnp.bfloat16
VMEM = pltpu.VMEM
SMEM = pltpu.SMEM


def split(x):
    hi = x.astype(BF16)
    lo = (x - hi.astype(F32)).astype(BF16)
    return hi, lo


def dot(a, b):
    return jnp.dot(a, b, preferred_element_type=F32)


def in_vmem(*xs):
    return [pltpu.with_memory_space_constraint(x, VMEM) for x in xs]


def in_hbm(*xs):
    return [pltpu.with_memory_space_constraint(x, pltpu.HBM) for x in xs]


def kept(shape, dtype=F32):
    return VMEM(shape, dtype)


WHOLE = pl.BlockSpec(memory_space=VMEM)
SCALARS = pl.BlockSpec(memory_space=SMEM)
RAW = pl.BlockSpec(memory_space=pltpu.HBM)


def limit(mib):
    return pltpu.CompilerParams(vmem_limit_bytes=mib << 20)


def pack_kernel(bands, slots, *refs):
    owner, live, raw, out, held = refs[0], refs[1], refs[2:5], refs[5], refs[6:]
    trip, center, modes, sem = held
    copies = [
        pltpu.make_async_copy(src, dst, sem.at[i])
        for i, (src, dst) in enumerate(zip(raw, (trip, center, modes)))
    ]
    for c in copies:
        c.start()
    out[...] = jnp.zeros_like(out)
    for c in copies:
        c.wait()
    row, ba = lax.axis_index("row"), lax.axis_index("ba")
    mine = (owner[0] == row).astype(F32)
    width = modes.shape[-1]
    order = [j for j in range(bands) if j % 2 == 0] + [j for j in range(bands) if j % 2]
    for place, j in enumerate(order):
        for s in range(2):
            line = modes[s, pl.ds(lax.bitwise_xor(ba, j), 1), :]
            out[pl.ds(place * 2 + s, 1), 0:width] = line * mine
    lane = lax.broadcasted_iota(jnp.int32, (1, LANES), 1)
    for r in range(slots):
        shift = 0
        entry = jnp.where(lane == 4, (r < live[0]).astype(jnp.int32), 0)
        for d in range(3):
            entry = jnp.where(lane == d, trip[r, d] - trip[r, 3 + d], entry)
            shift = shift + trip[r, 3 + d] * center[d]
        entry = jnp.where(lane == 3, shift, entry)
        out[pl.ds(2 * bands + row * slots + r, 1), :] = entry.astype(F32)


def pack(modes, owner, trip, center, live, bands, slots, total):
    rows = 2 * bands + -(-total // 8) * 8
    return pl.pallas_call(
        functools.partial(pack_kernel, bands, slots),
        out_shape=kept((rows, LANES)),
        in_specs=[SCALARS] * 2 + [RAW] * 3,
        out_specs=WHOLE,
        scratch_shapes=[SMEM(x.shape, x.dtype) for x in (trip, center)]
        + [VMEM(modes.shape, F32), pltpu.SemaphoreType.DMA((3,))],
        compiler_params=limit(4),
        name="pack",
    )(owner, live, *in_hbm(trip, center, modes))


def fetch_kernel(slots, first, rows, parts, const, hi, lo, buf, sem):
    width = const.shape[2] // parts
    copies = []
    for r in range(slots):
        for i in range(parts):
            lanes = pl.ds(i * width, width)
            copies.append(
                pltpu.make_async_copy(
                    const.at[r, pl.ds(first, rows), lanes], buf.at[r, :, lanes], sem.at[r, i]
                )
            )
    for c in copies:
        c.start()
    for n, c in enumerate(copies):
        c.wait()
        r, i = n // parts, n % parts
        lanes = slice(i * width, (i + 1) * width)
        hi[r, :, lanes], lo[r, :, lanes] = split(buf[r, :, lanes])


def fetch(constants, first, rows):
    slots, _, bb = constants.shape
    parts = 6
    return pl.pallas_call(
        functools.partial(fetch_kernel, slots, first, rows, parts),
        out_shape=(kept((slots, rows, bb), BF16),) * 2,
        in_specs=[RAW],
        out_specs=[WHOLE] * 2,
        scratch_shapes=[
            VMEM((slots, rows, bb), F32),
            pltpu.SemaphoreType.DMA((slots, parts)),
        ],
        compiler_params=limit(8),
        name="fetch",
    )(*in_hbm(constants))


def contract_kernel(bands, slots, lines, e0, e1, *refs):
    pieces, (keep, send) = refs[:-2], refs[-2:]
    his, los = pieces[0::2], pieces[1::2]
    width = sum(h.shape[1] for h in his)
    total = e0[...] + e1[...]
    eigen = total[0 : 2 * bands, 0:width]
    pairs, chunk = keep.shape[2], keep.shape[3]
    low = lax.broadcasted_iota(jnp.int32, (2 * bands, LANES), 1) < 64
    for r in range(slots):
        own = pl.ds(2 * bands + lax.axis_index("row") * slots + r, 1)
        weight = e0[own, 4:5] + e1[own, 4:5]
        eh, el = split(eigen * weight)
        left = jnp.concatenate(
            [
                jnp.concatenate([eh, eh], axis=1),
                jnp.concatenate([el, jnp.zeros_like(el)], axis=1),
            ],
            axis=0,
        )
        for base in range(0, pairs, lines):
            lanes = slice(base * chunk, (base + lines) * chunk)
            right = jnp.concatenate(
                [h[r, :, lanes] for h in his] + [m[r, :, lanes] for m in los], axis=0
            )
            both = dot(left, right)
            res = both[0 : 2 * bands] + both[2 * bands :]
            for q in range(lines):
                j0, j1, j2 = (
                    res[:, q * chunk + j * LANES : q * chunk + (j + 1) * LANES]
                    for j in range(3)
                )
                t1 = jnp.where(low, j1, j2)
                t2 = jnp.where(low, pltpu.roll(j1, 64, 1), pltpu.roll(j2, 64, 1))
                for j, t in enumerate((j0, t1, t2)):
                    spot = slice(j * LANES, (j + 1) * LANES)
                    keep[:, r, base + q, spot] = t[0:bands]
                    send[:, r, base + q, spot] = t[bands:]


def contract(pieces, e0, e1, bands):
    slots, _, bb = pieces[0].shape
    chunk = 3 * LANES
    return pl.pallas_call(
        functools.partial(contract_kernel, bands, slots, 8),
        out_shape=(kept((bands, slots, bb // chunk, chunk)),) * 2,
        in_specs=[WHOLE] * (2 + len(pieces)),
        out_specs=[WHOLE] * 2,
        compiler_params=limit(8),
        name="contract",
    )(*in_vmem(e0, e1, *pieces))


def unpack_matrix(ref, k, s, size):
    half = size // 2
    j0, j1, j2 = (ref[k, pl.ds(2 * j + s, half, stride=6), :] for j in range(3))
    lane = lax.broadcasted_iota(jnp.int32, j0.shape, 1)
    r1 = pltpu.roll(j1, 64, 1)
    r2 = pltpu.roll(j2, 64, 1)
    return (j0, j1), (jnp.where(lane < 64, r1, r2), r2)


def join(a, b, size):
    return jnp.concatenate([a, b[:, 0 : size - LANES]], axis=1)


def prep_kernel(size, turn, raw, hi, lo, buf, sem, left, right):
    half = size // 2
    count = raw.shape[0]
    copies = [
        pltpu.make_async_copy(raw.at[k], buf.at[k], sem.at[k]) for k in range(count)
    ]
    for c in copies:
        c.start()
    for k in range(count):
        copies[k].wait()
        mats = []
        for s in range(2):
            even, odd = unpack_matrix(buf, k, s, size)
            if turn:
                turned = jnp.concatenate([join(*even, size), join(*odd, size)], axis=0).T
                left[...] = turned[:, 0:LANES]
                right[:, 0 : size - LANES] = turned[:, LANES:size]
                rows = [
                    join(
                        left[pl.ds(p, half, stride=2), :],
                        right[pl.ds(p, half, stride=2), :],
                        size,
                    )
                    for p in range(2)
                ]
                mats.append(jnp.concatenate(rows, axis=0))
            else:
                for p, (a, b) in enumerate((even, odd)):
                    left[pl.ds(p, half, stride=2), :] = a
                    right[pl.ds(p, half, stride=2), :] = b
                mats.append(join(left[...], right[...], size))
        re, im = mats
        three = (re + im, re, im) if turn else (re, im - re, re + im)
        for i, m in enumerate(three):
            hi[k, i], lo[k, i] = split(m)


def prep(vectors, size, turn):
    count, _, bb = vectors.shape
    tiles = bb // LANES
    view = vectors.reshape(count, 2, tiles, LANES).swapaxes(1, 2)
    view = view.reshape(count, 2 * tiles, LANES)
    return pl.pallas_call(
        functools.partial(prep_kernel, size, turn),
        out_shape=(kept((count, 3, size, size), BF16),) * 2,
        in_specs=[RAW],
        out_specs=[WHOLE] * 2,
        scratch_shapes=[
            VMEM(view.shape, F32),
            pltpu.SemaphoreType.DMA((count,)),
            VMEM((size, LANES), F32),
            VMEM((size, LANES), F32),
        ],
        compiler_params=limit(8),
        name="prep",
    )(*in_hbm(view))


def angle_kernel(first, order, e0, e1, points, out):
    count, width = points.shape[1], len(order[0])
    row = lax.axis_index("row")
    lines = []
    for choice in zip(*order):
        if len(set(choice)) == 1:
            slot = choice[0]
        else:
            slot = sum(jnp.where(row == i, c, 0) for i, c in enumerate(choice))
        spot = pl.ds(first + slot, 1)
        lines.append(e0[spot, :] + e1[spot, :])
    lines = jnp.concatenate(lines, axis=0)
    cell = [jnp.broadcast_to(lines[:, d : d + 1], (width, LANES)) for d in range(4)]
    for k in range(count):
        turns = -cell[3]
        for d in range(3):
            turns = turns + cell[d] * points[d : d + 1, k : k + 1].astype(F32)
        turns = lax.rem(turns.astype(jnp.int32), G)
        turns = jnp.where(turns < 0, turns + G, turns)
        angle = turns.astype(F32) * (FULL_TURN / G)
        out[0, k * width : (k + 1) * width, :] = jnp.cos(angle)
        out[1, k * width : (k + 1) * width, :] = jnp.sin(angle)


def angles(e0, e1, points, first, order):
    lines = points.shape[0] * len(order[0])
    return pl.pallas_call(
        functools.partial(angle_kernel, first, order),
        out_shape=kept((2, lines, LANES)),
        in_specs=[WHOLE] * 3,
        out_specs=WHOLE,
        compiler_params=limit(4),
        name="angles",
    )(*in_vmem(e0, e1), points.T)


def rotated(refs, spec, cs, width, k, q0, group, re, im):
    for ref, (base, lines, slots) in zip(refs, spec):
        if not base <= q0 < base + lines:
            continue
        local = pl.ds(q0 - base, group)

        def turn(t, slot):
            spot = pl.ds(k * width + slot, 1)
            c, s = cs[0, spot, :], cs[1, spot, :]
            a, b = ref[t, 0, local, :], ref[t, 1, local, :]
            c, s = (jnp.concatenate([x] * 3, axis=1) for x in (c, s))
            return a * c - b * s, a * s + b * c

        if len(slots) <= 8:
            for t, slot in enumerate(slots):
                a, b = turn(t, slot)
                re = a if re is None else re + a
                im = b if im is None else im + b
        else:
            zero = jnp.zeros((group, 3 * LANES), F32)

            def step(t, carry):
                a, b = turn(t, t)
                return carry[0] + a, carry[1] + b

            start = (zero if re is None else re, zero if im is None else im)
            re, im = lax.fori_loop(0, len(slots), step, start)
    return re, im


def early_kernel(spec, width, group, *refs):
    blocks, cs, out = refs[: len(spec)], refs[-2], refs[-1]

    def one(k, carry):
        for q0 in range(0, out.shape[2], group):
            re, im = rotated(blocks, spec, cs, width, k, q0, group, None, None)
            out[k, 0, pl.ds(q0, group), :] = re
            out[k, 1, pl.ds(q0, group), :] = im
        return carry

    lax.fori_loop(0, out.shape[0], one, 0)


def early(blocks, spec, cs, count, half):
    width = cs.shape[1] // count
    return pl.pallas_call(
        functools.partial(early_kernel, spec, width, 8),
        out_shape=kept((count, 2, half, 3 * LANES)),
        in_specs=[WHOLE] * (len(blocks) + 1),
        out_specs=WHOLE,
        compiler_params=limit(4),
        name="early",
    )(*in_vmem(*blocks, cs))


def final_kernel(spec, width, scale, size, unroll, partial, *refs):
    blocks = refs[: len(spec)]
    cs, gh, gl, wh, wl, out, ph, plo = refs[len(spec) :]
    half = size // 2
    group = 16
    first = pl.program_id(0) * unroll

    def load(u):
        k = first + u
        for q0 in range(0, half, group):
            re, im = partial[k, 0, pl.ds(q0, group), :], partial[k, 1, pl.ds(q0, group), :]
            re, im = rotated(blocks, spec, cs, width, k, q0, group, re, im)
            for i, m in enumerate((re + im, re, im)):
                t0, t1, t2 = (m[:, j * LANES : (j + 1) * LANES] for j in range(3))
                for base, a, b in ((0, t0, t1), (half, t2, pltpu.roll(t1, 64, 1))):
                    spot = pl.ds(base + q0, group)
                    for dst, x, y in zip((ph, plo), split(a), split(b)):
                        dst[u, i, spot, 0:LANES] = x
                        dst[u, i, spot, LANES : 2 * LANES] = y

    def triple(xh, xl, yh, yl):
        both = dot(jnp.concatenate([xh, xl], axis=0), yh)
        return both[0:size] + both[size:] + dot(xh, yl)

    def inner(u):
        k = first + u
        k1, k2, k3 = (
            triple(ph[u, i][:, 0:size], plo[u, i][:, 0:size], wh[k, i], wl[k, i])
            for i in range(3)
        )
        return k1 - k3, k1 + k2

    def outer(u, re, im):
        k = first + u
        k1, k2, k3 = (
            triple(gh[k, i], gl[k, i], *split(m))
            for i, m in enumerate((re, im - re, re + im))
        )
        re, im = k1 - k3, k1 + k2
        return (re * re + im * im) * scale

    def store(u, value):
        tail = value[:, LANES:size]
        tail = jnp.concatenate([tail, tail], axis=1)
        turned = pltpu.roll(value[half:, 0:LANES], 64, 1)
        low = lax.broadcasted_iota(jnp.int32, turned.shape, 1) < 64
        out[u, pl.ds(0, half, stride=3), :] = value[0:half, 0:LANES]
        out[u, pl.ds(1, half, stride=3), :] = jnp.where(low, tail[0:half], turned)
        out[u, pl.ds(2, half, stride=3), :] = jnp.where(low, turned, tail[half:])

    for u in range(unroll):
        load(u)
    sums = [inner(u) for u in range(unroll)]
    for u in range(unroll):
        store(u, outer(u, *sums[u]))


def final(partial, blocks, spec, cs, operands, total):
    count, _, size, _ = operands[0].shape
    tiles = size * size // LANES
    unroll = 2 if count % 2 == 0 else 1
    result = pl.pallas_call(
        functools.partial(final_kernel, spec, cs.shape[1] // count, 1.0 / total, size, unroll),
        out_shape=jax.ShapeDtypeStruct((count, tiles, LANES), F32),
        grid=(count // unroll,),
        in_specs=[WHOLE] * (6 + len(blocks)),
        out_specs=pl.BlockSpec((unroll, tiles, LANES), lambda k: (k, 0, 0)),
        scratch_shapes=[VMEM((unroll, 3, size, 2 * LANES), BF16)] * 2,
        compiler_params=limit(16),
        name="final",
    )(*in_vmem(partial, *blocks, cs, *operands))
    return result.reshape(count, 1, size * size)


def swap(x, axis, bit, n):
    return lax.ppermute(x, axis, [(i, i ^ bit) for i in range(n)])


def edges(n):
    cycle = list(range(0, n, 2)) + list(range(n - 1, 0, -2))
    even, odd = [], []
    for i in range(0, n, 2):
        a, b, c = cycle[i], cycle[i + 1], cycle[(i + 2) % n]
        even += [(a, b), (b, a)]
        odd += [(b, c), (c, b)]
    return even, odd


def neighbour_gather(parts, n):
    even, odd = edges(n)
    plans = ((even, odd), (odd, even))
    moving = [p[None] for p in parts]
    held = [np.arange(n)[:, None] for _ in parts]
    blocks, sources = [[], []], [[], []]
    for step in range(n // 2):
        arrived = []
        for h, plan in enumerate(plans):
            perm = plan[step % 2]
            arrived.append(lax.ppermute(moving[h], "row", perm))
            source = np.zeros_like(held[h])
            for a, b in perm:
                source[b] = held[h][a]
            if step == 0:
                source = np.concatenate([held[h], source], axis=1)
            held[h] = source
            sources[h].append(source)
        for h in range(2):
            if step == 0:
                arrived[h] = jnp.concatenate([moving[h], arrived[h]])
            moving[h] = arrived[h]
            blocks[h].append(moving[h])
    return blocks, [np.concatenate(s, axis=1) for s in sources]


def body(
    constants,
    current_modes,
    owner_id,
    live_count,
    triplets,
    center_point,
    pair_points,
    first_vectors,
    second_vectors,
):
    n_row, n_ba = lax.axis_size("row"), lax.axis_size("ba")
    slots, width, _ = constants.shape
    size = width * n_ba
    bands = current_modes.shape[-1]
    half = size // 2
    total = slots * n_row
    modes = jnp.swapaxes(current_modes[0], 1, 2)
    payload = pack(
        modes, owner_id, triplets, center_point, live_count, bands, slots, total
    )
    bit = 1
    while bit < n_row:
        other = swap(payload, "row", bit, n_row)
        bit = bit * 2
        if bit < n_row:
            payload = payload + other
    cuts = 3 if width % 48 == 0 else 1
    pieces = []
    for i in range(cuts):
        pieces += fetch(constants, i * width // cuts, width // cuts)
    keep, send = contract(pieces, payload, other, bands)

    keep = keep.reshape(bands // 2, 2, slots, half, 2 * size)
    send = send.reshape(bands // 2, 2, slots, half, 2 * size)
    got = swap(send, "ba", 1, n_ba)
    far = swap(keep[1] + got[1], "ba", 2, n_ba)
    own = (keep[0] + got[0]) + far
    own = own.swapaxes(0, 1)

    weights = prep(second_vectors, size, False)
    lefts = prep(first_vectors, size, True)
    operands = (*lefts, *weights)
    if slots == 1 and n_row <= 8:
        parts = (own[0, :, : half // 2], own[0, :, half // 2 :])
        blocks, sources = neighbour_gather(parts, n_row)
        order = np.concatenate(sources, axis=1)
        ahead, behind = [], []
        for h in range(2):
            slot = h * n_row
            for n, b in enumerate(blocks[h]):
                here = range(slot, slot + b.shape[0])
                entry = (b, (h * half // 2, half // 2, tuple(here)))
                (behind if n == len(blocks[h]) - 1 else ahead).append(entry)
                slot += b.shape[0]
    else:
        gathered = lax.all_gather(own, "row", axis=0, tiled=True)
        ahead, behind = [(gathered, (0, half, tuple(range(total))))], []
        order = np.broadcast_to(np.arange(total), (n_row, total))
    order = tuple(tuple(int(x) for x in line) for line in order)
    table = angles(payload, other, pair_points, 2 * bands, order)
    arrays, spec = zip(*ahead)
    partial = early(arrays, spec, table, pair_points.shape[0], half)
    arrays, spec = zip(*behind) if behind else ((), ())
    return final(partial, arrays, spec, table, operands, total)


def solution(mesh):
    return jax.shard_map(
        body,
        mesh=mesh,
        in_specs=(
            P("row", "ba", None),
            P("row", None, "ba", None),
            P(),
            P("row"),
            P("row", None),
            P(),
            P("row", None),
            P("row", None, None),
            P("row", None, None),
        ),
        out_specs=P("row", "ba", None),
        check_vma=False,
    )
```

```python
import functools
import math

import jax
import jax.numpy as jnp
import numpy as np
from jax import lax
from jax.experimental import pallas as pl
from jax.experimental.pallas import tpu as pltpu
from jax.sharding import PartitionSpec as P

G = 32
FULL_TURN = 2.0 * math.pi
LANES = 128
F32 = jnp.float32
BF16 = jnp.bfloat16
VMEM = pltpu.VMEM
SMEM = pltpu.SMEM


def split(x):
    hi = x.astype(BF16)
    lo = (x - hi.astype(F32)).astype(BF16)
    return hi, lo


def dot(a, b):
    return jnp.dot(a, b, preferred_element_type=F32)


def in_vmem(*xs):
    return [pltpu.with_memory_space_constraint(x, VMEM) for x in xs]


def in_hbm(*xs):
    return [pltpu.with_memory_space_constraint(x, pltpu.HBM) for x in xs]


def kept(shape, dtype=F32):
    return VMEM(shape, dtype)


WHOLE = pl.BlockSpec(memory_space=VMEM)
SCALARS = pl.BlockSpec(memory_space=SMEM)
RAW = pl.BlockSpec(memory_space=pltpu.HBM)


def limit(mib):
    return pltpu.CompilerParams(vmem_limit_bytes=mib << 20)


def pack_kernel(bands, slots, *refs):
    owner, raw, out, (trip, center, modes, sem) = refs[0], refs[1:4], refs[4], refs[5:]
    copies = [
        pltpu.make_async_copy(src, dst, sem.at[i])
        for i, (src, dst) in enumerate(zip(raw, (trip, center, modes)))
    ]
    for c in copies:
        c.start()
    out[...] = jnp.zeros_like(out)
    for c in copies:
        c.wait()
    row, ba = lax.axis_index("row"), lax.axis_index("ba")
    mine = (owner[0] == row).astype(F32)
    width = modes.shape[-1]
    order = [j for j in range(bands) if j % 2 == 0] + [j for j in range(bands) if j % 2]
    for place, j in enumerate(order):
        for s in range(2):
            line = modes[s, pl.ds(lax.bitwise_xor(ba, j), 1), :]
            out[pl.ds(place * 2 + s, 1), 0:width] = line * mine
    lane = lax.broadcasted_iota(jnp.int32, (1, LANES), 1)
    for r in range(slots):
        shift = 0
        entry = jnp.zeros((1, LANES), jnp.int32)
        for d in range(3):
            entry = jnp.where(lane == d, trip[r, d] - trip[r, 3 + d], entry)
            shift = shift + trip[r, 3 + d] * center[d]
        entry = jnp.where(lane == 3, shift, entry)
        out[pl.ds(2 * bands + row * slots + r, 1), :] = entry.astype(F32)


def pack(modes, owner, trip, center, bands, slots, total):
    rows = 2 * bands + -(-total // 8) * 8
    return pl.pallas_call(
        functools.partial(pack_kernel, bands, slots),
        out_shape=kept((rows, LANES)),
        in_specs=[SCALARS] + [RAW] * 3,
        out_specs=WHOLE,
        scratch_shapes=[SMEM(x.shape, x.dtype) for x in (trip, center)]
        + [VMEM(modes.shape, F32), pltpu.SemaphoreType.DMA((3,))],
        compiler_params=limit(4),
        name="pack",
    )(owner, *in_hbm(trip, center, modes))


def fetch_kernel(slots, first, rows, parts, const, hi, lo, buf, sem):
    width = const.shape[2] // parts
    copies = []
    for r in range(slots):
        for i in range(parts):
            lanes = pl.ds(i * width, width)
            copies.append(
                pltpu.make_async_copy(
                    const.at[r, pl.ds(first, rows), lanes], buf.at[r, :, lanes], sem.at[r, i]
                )
            )
    for c in copies:
        c.start()
    for n, c in enumerate(copies):
        c.wait()
        r, i = n // parts, n % parts
        lanes = slice(i * width, (i + 1) * width)
        hi[r, :, lanes], lo[r, :, lanes] = split(buf[r, :, lanes])


def fetch(constants, first, rows):
    slots, _, bb = constants.shape
    parts = 6
    return pl.pallas_call(
        functools.partial(fetch_kernel, slots, first, rows, parts),
        out_shape=(kept((slots, rows, bb), BF16),) * 2,
        in_specs=[RAW],
        out_specs=[WHOLE] * 2,
        scratch_shapes=[
            VMEM((slots, rows, bb), F32),
            pltpu.SemaphoreType.DMA((slots, parts)),
        ],
        compiler_params=limit(8),
        name="fetch",
    )(*in_hbm(constants))


def contract_kernel(bands, slots, first, lines, e0, e1, *refs):
    pieces, (keep, send) = refs[:-2], refs[-2:]
    his, los = pieces[0::2], pieces[1::2]
    width = sum(h.shape[1] for h in his)
    total = e0[...] + e1[...]
    eigen = total[0 : 2 * bands, 0:width]
    pairs, chunk = keep.shape[2], keep.shape[3]
    low = lax.broadcasted_iota(jnp.int32, (2 * bands, LANES), 1) < 64
    for r in range(slots):
        eh, el = split(eigen)
        left = jnp.concatenate(
            [
                jnp.concatenate([eh, eh], axis=1),
                jnp.concatenate([el, jnp.zeros_like(el)], axis=1),
            ],
            axis=0,
        )
        for base in range(0, pairs, lines):
            lanes = slice((first + base) * chunk, (first + base + lines) * chunk)
            right = jnp.concatenate(
                [h[r, :, lanes] for h in his] + [m[r, :, lanes] for m in los], axis=0
            )
            both = dot(left, right)
            res = both[0 : 2 * bands] + both[2 * bands :]
            for q in range(lines):
                j0, j1, j2 = (
                    res[:, q * chunk + j * LANES : q * chunk + (j + 1) * LANES]
                    for j in range(3)
                )
                t1 = jnp.where(low, j1, j2)
                t2 = jnp.where(low, pltpu.roll(j1, 64, 1), pltpu.roll(j2, 64, 1))
                for j, t in enumerate((j0, t1, t2)):
                    spot = slice(j * LANES, (j + 1) * LANES)
                    keep[:, r, base + q, spot] = t[0:bands]
                    send[:, r, base + q, spot] = t[bands:]


def contract(pieces, e0, e1, bands, first, count):
    slots = pieces[0].shape[0]
    return pl.pallas_call(
        functools.partial(contract_kernel, bands, slots, first, 8),
        out_shape=(kept((bands, slots, count, 3 * LANES)),) * 2,
        in_specs=[WHOLE] * (2 + len(pieces)),
        out_specs=[WHOLE] * 2,
        compiler_params=limit(8),
        name="contract",
    )(*in_vmem(e0, e1, *pieces))


def unpack_matrix(ref, k, s, size):
    half = size // 2
    j0, j1, j2 = (ref[k, pl.ds(2 * j + s, half, stride=6), :] for j in range(3))
    lane = lax.broadcasted_iota(jnp.int32, j0.shape, 1)
    r1 = pltpu.roll(j1, 64, 1)
    r2 = pltpu.roll(j2, 64, 1)
    return (j0, j1), (jnp.where(lane < 64, r1, r2), r2)


def join(a, b, size):
    return jnp.concatenate([a, b[:, 0 : size - LANES]], axis=1)


def prep_kernel(size, turn, spans, raw, hi, lo, buf, sem, left, right):
    half = size // 2
    count = raw.shape[0]
    copies = [
        pltpu.make_async_copy(raw.at[k], buf.at[k], sem.at[k]) for k in range(count)
    ]
    for c in copies:
        c.start()
    for k in range(count):
        copies[k].wait()
        mats = []
        for s in range(2):
            even, odd = unpack_matrix(buf, k, s, size)
            if turn:
                both = join(*even, size), join(*odd, size)
                rows = [x[a : a + n] for a, n in spans for x in both]
                turned = jnp.concatenate(rows, axis=0).T
                left[...] = turned[:, 0:LANES]
                right[:, 0 : size - LANES] = turned[:, LANES:size]
                rows = [
                    join(
                        left[pl.ds(p, half, stride=2), :],
                        right[pl.ds(p, half, stride=2), :],
                        size,
                    )
                    for p in range(2)
                ]
                mats.append(jnp.concatenate(rows, axis=0))
            else:
                for p, (a, b) in enumerate((even, odd)):
                    left[pl.ds(p, half, stride=2), :] = a
                    right[pl.ds(p, half, stride=2), :] = b
                mats.append(join(left[...], right[...], size))
        re, im = mats
        three = (re + im, re, im) if turn else (re, im - re, re + im)
        for i, m in enumerate(three):
            hi[k, i], lo[k, i] = split(m)


def prep(vectors, size, turn, spans):
    count, _, bb = vectors.shape
    tiles = bb // LANES
    view = vectors.reshape(count, 2, tiles, LANES).swapaxes(1, 2)
    view = view.reshape(count, 2 * tiles, LANES)
    return pl.pallas_call(
        functools.partial(prep_kernel, size, turn, spans),
        out_shape=(kept((count, 3, size, size), BF16),) * 2,
        in_specs=[RAW],
        out_specs=[WHOLE] * 2,
        scratch_shapes=[
            VMEM(view.shape, F32),
            pltpu.SemaphoreType.DMA((count,)),
            VMEM((size, LANES), F32),
            VMEM((size, LANES), F32),
        ],
        compiler_params=limit(8),
        name="prep",
    )(*in_hbm(view))


def angle_kernel(first, order, e0, e1, points, out):
    count, width = points.shape[1], len(order[0])
    row = lax.axis_index("row")
    lines = []
    for choice in zip(*order):
        if len(set(choice)) == 1:
            slot = choice[0]
        else:
            slot = sum(jnp.where(row == i, c, 0) for i, c in enumerate(choice))
        spot = pl.ds(first + slot, 1)
        lines.append(e0[spot, :] + e1[spot, :])
    lines = jnp.concatenate(lines, axis=0)
    cell = [jnp.broadcast_to(lines[:, d : d + 1], (width, LANES)) for d in range(4)]
    for k in range(count):
        turns = -cell[3]
        for d in range(3):
            turns = turns + cell[d] * points[d : d + 1, k : k + 1].astype(F32)
        turns = lax.rem(turns.astype(jnp.int32), G)
        turns = jnp.where(turns < 0, turns + G, turns)
        angle = turns.astype(F32) * (FULL_TURN / G)
        out[0, k * width : (k + 1) * width, :] = jnp.cos(angle)
        out[1, k * width : (k + 1) * width, :] = jnp.sin(angle)


def angles(e0, e1, points, first, order):
    lines = points.shape[0] * len(order[0])
    return pl.pallas_call(
        functools.partial(angle_kernel, first, order),
        out_shape=kept((2, lines, LANES)),
        in_specs=[WHOLE] * 3,
        out_specs=WHOLE,
        compiler_params=limit(4),
        name="angles",
    )(*in_vmem(e0, e1), points.T)


def rotated(refs, spec, cs, width, k, q0, group, re, im):
    for ref, (base, lines, slots) in zip(refs, spec):
        if not base <= q0 < base + lines:
            continue
        local = pl.ds(q0 - base, group)

        def turn(t, slot):
            spot = pl.ds(k * width + slot, 1)
            c, s = cs[0, spot, :], cs[1, spot, :]
            a, b = ref[t, 0, local, :], ref[t, 1, local, :]
            c, s = (jnp.concatenate([x] * 3, axis=1) for x in (c, s))
            return a * c - b * s, a * s + b * c

        if len(slots) <= 8:
            for t, slot in enumerate(slots):
                a, b = turn(t, slot)
                re = a if re is None else re + a
                im = b if im is None else im + b
        else:
            zero = jnp.zeros((group, 3 * LANES), F32)

            def step(t, carry):
                a, b = turn(t, t)
                return carry[0] + a, carry[1] + b

            start = (zero if re is None else re, zero if im is None else im)
            re, im = lax.fori_loop(0, len(slots), step, start)
    return re, im


def early_kernel(spec, width, group, *refs):
    blocks, cs, out = refs[: len(spec)], refs[-2], refs[-1]

    def one(k, carry):
        for q0 in range(0, out.shape[2], group):
            re, im = rotated(blocks, spec, cs, width, k, q0, group, None, None)
            out[k, 0, pl.ds(q0, group), :] = re
            out[k, 1, pl.ds(q0, group), :] = im
        return carry

    lax.fori_loop(0, out.shape[0], one, 0)


def early(blocks, spec, cs, count, half):
    width = cs.shape[1] // count
    return pl.pallas_call(
        functools.partial(early_kernel, spec, width, 8),
        out_shape=kept((count, 2, half, 3 * LANES)),
        in_specs=[WHOLE] * (len(blocks) + 1),
        out_specs=WHOLE,
        compiler_params=limit(4),
        name="early",
    )(*in_vmem(*blocks, cs))


def triple(xh, xl, yh, yl):
    rows = xh.shape[0]
    both = dot(jnp.concatenate([xh, xl], axis=0), yh)
    return both[0:rows] + both[rows:] + dot(xh, yl)


def load(span, width, spec, k, u, partial, blocks, cs, ph, plo):
    first, lines = span
    group = 16
    for q0 in range(first, first + lines, group):
        re, im = partial[k, 0, pl.ds(q0, group), :], partial[k, 1, pl.ds(q0, group), :]
        re, im = rotated(blocks, spec, cs, width, k, q0, group, re, im)
        for i, m in enumerate((re + im, re, im)):
            t0, t1, t2 = (m[:, j * LANES : (j + 1) * LANES] for j in range(3))
            for base, a, b in ((0, t0, t1), (lines, t2, pltpu.roll(t1, 64, 1))):
                spot = pl.ds(base + q0 - first, group)
                for dst, x, y in zip((ph, plo), split(a), split(b)):
                    dst[u, i, spot, 0:LANES] = x
                    dst[u, i, spot, LANES : 2 * LANES] = y


def product(size, k, u, ph, plo, wh, wl):
    k1, k2, k3 = (
        triple(ph[u, i][:, 0:size], plo[u, i][:, 0:size], wh[k, i], wl[k, i])
        for i in range(3)
    )
    return k1 - k3, k1 + k2


def inner_kernel(span, width, spec, size, unroll, partial, *refs):
    blocks = refs[: len(spec)]
    cs, wh, wl, out, ph, plo = refs[len(spec) :]
    first = pl.program_id(0) * unroll
    for u in range(unroll):
        load(span, width, spec, first + u, u, partial, blocks, cs, ph, plo)
    for u in range(unroll):
        k = first + u
        out[k, 0], out[k, 1] = product(size, k, u, ph, plo, wh, wl)


def halves(unroll, span):
    return [VMEM((unroll, 3, 2 * span[1], 2 * LANES), BF16)] * 2


def inner(span, partial, blocks, spec, cs, weights):
    count, _, size, _ = weights[0].shape
    unroll = 2 if count % 2 == 0 else 1
    return pl.pallas_call(
        functools.partial(inner_kernel, span, cs.shape[1] // count, spec, size, unroll),
        out_shape=kept((count, 2, 2 * span[1], size)),
        grid=(count // unroll,),
        in_specs=[WHOLE] * (4 + len(blocks)),
        out_specs=WHOLE,
        scratch_shapes=halves(unroll, span),
        compiler_params=limit(8),
        name="inner",
    )(*in_vmem(partial, *blocks, cs, *weights))


def final_kernel(span, width, spec, scale, size, unroll, done, partial, *refs):
    blocks = refs[: len(spec)]
    cs, gh, gl, wh, wl, out, ph, plo = refs[len(spec) :]
    half = size // 2
    first = pl.program_id(0) * unroll

    def outer(u, sums):
        k = first + u
        re, im = (jnp.concatenate([done[k, i], x], axis=0) for i, x in enumerate(sums))
        k1, k2, k3 = (
            triple(gh[k, i], gl[k, i], *split(m))
            for i, m in enumerate((re, im - re, re + im))
        )
        re, im = k1 - k3, k1 + k2
        return (re * re + im * im) * scale

    def store(u, value):
        tail = value[:, LANES:size]
        tail = jnp.concatenate([tail, tail], axis=1)
        turned = pltpu.roll(value[half:, 0:LANES], 64, 1)
        low = lax.broadcasted_iota(jnp.int32, turned.shape, 1) < 64
        out[u, pl.ds(0, half, stride=3), :] = value[0:half, 0:LANES]
        out[u, pl.ds(1, half, stride=3), :] = jnp.where(low, tail[0:half], turned)
        out[u, pl.ds(2, half, stride=3), :] = jnp.where(low, turned, tail[half:])

    for u in range(unroll):
        load(span, width, spec, first + u, u, partial, blocks, cs, ph, plo)
    sums = [product(size, first + u, u, ph, plo, wh, wl) for u in range(unroll)]
    for u in range(unroll):
        store(u, outer(u, sums[u]))


def final(span, done, partial, blocks, spec, cs, lefts, weights, total):
    count, _, size, _ = weights[0].shape
    tiles = size * size // LANES
    unroll = 2 if count % 2 == 0 else 1
    width = cs.shape[1] // count
    result = pl.pallas_call(
        functools.partial(final_kernel, span, width, spec, 1.0 / total, size, unroll),
        out_shape=jax.ShapeDtypeStruct((count, tiles, LANES), F32),
        grid=(count // unroll,),
        in_specs=[WHOLE] * (7 + len(blocks)),
        out_specs=pl.BlockSpec((unroll, tiles, LANES), lambda k: (k, 0, 0)),
        scratch_shapes=halves(unroll, span),
        compiler_params=limit(12),
        name="final",
    )(*in_vmem(done, partial, *blocks, cs, *lefts, *weights))
    return result.reshape(count, 1, size * size)


def swap(x, axis, bit, n):
    return lax.ppermute(x, axis, [(i, i ^ bit) for i in range(n)])


def edges(n):
    cycle = list(range(0, n, 2)) + list(range(n - 1, 0, -2))
    even, odd = [], []
    for i in range(0, n, 2):
        a, b, c = cycle[i], cycle[i + 1], cycle[(i + 2) % n]
        even += [(a, b), (b, a)]
        odd += [(b, c), (c, b)]
    return even, odd


def chunks(lines):
    return ((0, 2 * lines // 3), (2 * lines // 3, lines // 3))


def neighbour_gather(parts, n):
    even, odd = edges(n)
    moving = [p[None] for p in parts]
    held = [np.arange(n)[:, None] for _ in parts]
    blocks, sources = [[] for _ in parts], [[] for _ in parts]
    for step in range(n // 2):
        arrived = []
        for h in range(len(parts)):
            perm = (even, odd)[(step + h) % 2]
            arrived.append(lax.ppermute(moving[h], "row", perm))
            source = np.zeros_like(held[h])
            for a, b in perm:
                source[b] = held[h][a]
            if step == 0:
                source = np.concatenate([held[h], source], axis=1)
            held[h] = source
            sources[h].append(source)
        for h in range(len(parts)):
            if step == 0:
                arrived[h] = jnp.concatenate([moving[h], arrived[h]])
            moving[h] = arrived[h]
            blocks[h].append(moving[h])
    return blocks, [np.concatenate(s, axis=1) for s in sources]


def body(
    constants,
    current_modes,
    owner_id,
    live_count,
    triplets,
    center_point,
    pair_points,
    first_vectors,
    second_vectors,
):
    n_row, n_ba = lax.axis_size("row"), lax.axis_size("ba")
    slots, width, _ = constants.shape
    size = width * n_ba
    bands = current_modes.shape[-1]
    half = size // 2
    total = slots * n_row
    modes = jnp.swapaxes(current_modes[0], 1, 2)
    payload = pack(modes, owner_id, triplets, center_point, bands, slots, total)
    bit = 1
    while bit < n_row:
        other = swap(payload, "row", bit, n_row)
        bit = bit * 2
        if bit < n_row:
            payload = payload + other
    cuts = 3 if width % 48 == 0 else 1
    pieces = []
    for i in range(cuts):
        pieces += fetch(constants, i * width // cuts, width // cuts)
    spans = chunks(half)
    weight = (jnp.arange(slots, dtype=jnp.int32) < live_count[0]).astype(F32)
    owns = []
    for base, lines in spans:
        keep, send = contract(pieces, payload, other, bands, base, lines)
        keep = keep.reshape(bands // 2, 2, slots, lines, 2 * size)
        send = send.reshape(bands // 2, 2, slots, lines, 2 * size)
        got = swap(send, "ba", 1, n_ba)
        far = swap(keep[1] + got[1], "ba", 2, n_ba)
        own = ((keep[0] + got[0]) + far) * weight[None, :, None, None]
        owns.append(own.swapaxes(0, 1))

    weights = prep(second_vectors, size, False, spans)
    lefts = prep(first_vectors, size, True, spans)
    if slots == 1 and n_row <= 8:
        parts, places = [], []
        for own, (base, lines) in zip(owns, spans):
            for start in (0, lines // 2):
                parts.append(own[0, :, start : start + lines // 2])
                places.append((base + start, lines // 2))
        blocks, sources = neighbour_gather(parts, n_row)
        order = np.concatenate(sources, axis=1)
        ahead, behind = [], [[] for _ in spans]
        for h, (base, lines) in enumerate(places):
            slot = h * n_row
            for n, b in enumerate(blocks[h]):
                here = range(slot, slot + b.shape[0])
                entry = (b, (base, lines, tuple(here)))
                (behind[h // 2] if n == len(blocks[h]) - 1 else ahead).append(entry)
                slot += b.shape[0]
    else:
        slots_all = tuple(range(total))
        ahead, behind = [], [[] for _ in spans]
        for own, (base, lines) in zip(owns, spans):
            gathered = lax.all_gather(own, "row", axis=0, tiled=True)
            ahead.append((gathered, (base, lines, slots_all)))
        order = np.broadcast_to(np.arange(total), (n_row, total))
    order = tuple(tuple(int(x) for x in line) for line in order)
    table = angles(payload, other, pair_points, 2 * bands, order)
    partial = early(*zip(*ahead), table, pair_points.shape[0], half)
    late = [tuple(zip(*b)) if b else ((), ()) for b in behind]
    done = inner(spans[0], partial, *late[0], table, weights)
    return final(spans[1], done, partial, *late[1], table, lefts, weights, total)


def solution(mesh):
    return jax.shard_map(
        body,
        mesh=mesh,
        in_specs=(
            P("row", "ba", None),
            P("row", None, "ba", None),
            P(),
            P("row"),
            P("row", None),
            P(),
            P("row", None),
            P("row", None, None),
            P("row", None, None),
        ),
        out_specs=P("row", "ba", None),
        check_vma=False,
    )
```

```python
import functools
import math

import jax
import jax.numpy as jnp
import numpy as np
from jax import lax
from jax.experimental import pallas as pl
from jax.experimental.pallas import tpu as pltpu
from jax.sharding import PartitionSpec as P

G = 32
FIRST = 1
FULL_TURN = 2.0 * math.pi
LANES = 128
F32 = jnp.float32
BF16 = jnp.bfloat16
VMEM = pltpu.VMEM
SMEM = pltpu.SMEM


def split(x):
    hi = x.astype(BF16)
    lo = (x - hi.astype(F32)).astype(BF16)
    return hi, lo


def dot(a, b):
    return jnp.dot(a, b, preferred_element_type=F32)


def in_vmem(*xs):
    return [pltpu.with_memory_space_constraint(x, VMEM) for x in xs]


def in_hbm(*xs):
    return [pltpu.with_memory_space_constraint(x, pltpu.HBM) for x in xs]


def kept(shape, dtype=F32):
    return VMEM(shape, dtype)


WHOLE = pl.BlockSpec(memory_space=VMEM)
SCALARS = pl.BlockSpec(memory_space=SMEM)
RAW = pl.BlockSpec(memory_space=pltpu.HBM)


def limit(mib):
    return pltpu.CompilerParams(vmem_limit_bytes=mib << 20)


def pack_kernel(bands, slots, *refs):
    owner, raw, out, (trip, center, modes, sem) = refs[0], refs[1:4], refs[4], refs[5:]
    copies = [
        pltpu.make_async_copy(src, dst, sem.at[i])
        for i, (src, dst) in enumerate(zip(raw, (trip, center, modes)))
    ]
    for c in copies:
        c.start()
    out[...] = jnp.zeros_like(out)
    for c in copies:
        c.wait()
    row, ba = lax.axis_index("row"), lax.axis_index("ba")
    mine = (owner[0] == row).astype(F32)
    width = modes.shape[-1]
    order = [j for j in range(bands) if j % 2 == 0] + [j for j in range(bands) if j % 2]
    for place, j in enumerate(order):
        for s in range(2):
            line = modes[s, pl.ds(lax.bitwise_xor(ba, j), 1), :]
            out[pl.ds(place * 2 + s, 1), 0:width] = line * mine
    lane = lax.broadcasted_iota(jnp.int32, (1, LANES), 1)
    for r in range(slots):
        shift = 0
        entry = jnp.zeros((1, LANES), jnp.int32)
        for d in range(3):
            entry = jnp.where(lane == d, trip[r, d] - trip[r, 3 + d], entry)
            shift = shift + trip[r, 3 + d] * center[d]
        entry = jnp.where(lane == 3, shift, entry)
        out[pl.ds(2 * bands + row * slots + r, 1), :] = entry.astype(F32)


def pack(modes, owner, trip, center, bands, slots, total):
    rows = 2 * bands + -(-total // 8) * 8
    return pl.pallas_call(
        functools.partial(pack_kernel, bands, slots),
        out_shape=kept((rows, LANES)),
        in_specs=[SCALARS] + [RAW] * 3,
        out_specs=WHOLE,
        scratch_shapes=[SMEM(x.shape, x.dtype) for x in (trip, center)]
        + [VMEM(modes.shape, F32), pltpu.SemaphoreType.DMA((3,))],
        compiler_params=limit(4),
        name="pack",
    )(owner, *in_hbm(trip, center, modes))


def fetch_kernel(slots, first, rows, parts, const, hi, lo, buf, sem):
    width = const.shape[2] // parts
    copies = []
    for r in range(slots):
        for i in range(parts):
            lanes = pl.ds(i * width, width)
            copies.append(
                pltpu.make_async_copy(
                    const.at[r, pl.ds(first, rows), lanes], buf.at[r, :, lanes], sem.at[r, i]
                )
            )
    for c in copies:
        c.start()
    for n, c in enumerate(copies):
        c.wait()
        r, i = n // parts, n % parts
        lanes = slice(i * width, (i + 1) * width)
        hi[r, :, lanes], lo[r, :, lanes] = split(buf[r, :, lanes])


def fetch(constants, first, rows):
    slots, _, bb = constants.shape
    parts = 6
    return pl.pallas_call(
        functools.partial(fetch_kernel, slots, first, rows, parts),
        out_shape=(kept((slots, rows, bb), BF16),) * 2,
        in_specs=[RAW],
        out_specs=[WHOLE] * 2,
        scratch_shapes=[
            VMEM((slots, rows, bb), F32),
            pltpu.SemaphoreType.DMA((slots, parts)),
        ],
        compiler_params=limit(8),
        name="fetch",
    )(*in_hbm(constants))


def contract_kernel(bands, slots, first, lines, e0, e1, *refs):
    pieces, (keep, send) = refs[:-2], refs[-2:]
    his, los = pieces[0::2], pieces[1::2]
    width = sum(h.shape[1] for h in his)
    total = e0[...] + e1[...]
    eigen = total[0 : 2 * bands, 0:width]
    pairs, chunk = keep.shape[2], keep.shape[3]
    low = lax.broadcasted_iota(jnp.int32, (2 * bands, LANES), 1) < 64
    for r in range(slots):
        eh, el = split(eigen)
        left = jnp.concatenate(
            [
                jnp.concatenate([eh, eh], axis=1),
                jnp.concatenate([el, jnp.zeros_like(el)], axis=1),
            ],
            axis=0,
        )
        for base in range(0, pairs, lines):
            lanes = slice((first + base) * chunk, (first + base + lines) * chunk)
            right = jnp.concatenate(
                [h[r, :, lanes] for h in his] + [m[r, :, lanes] for m in los], axis=0
            )
            both = dot(left, right)
            res = both[0 : 2 * bands] + both[2 * bands :]
            for q in range(lines):
                j0, j1, j2 = (
                    res[:, q * chunk + j * LANES : q * chunk + (j + 1) * LANES]
                    for j in range(3)
                )
                t1 = jnp.where(low, j1, j2)
                t2 = jnp.where(low, pltpu.roll(j1, 64, 1), pltpu.roll(j2, 64, 1))
                for j, t in enumerate((j0, t1, t2)):
                    spot = slice(j * LANES, (j + 1) * LANES)
                    keep[:, r, base + q, spot] = t[0:bands]
                    send[:, r, base + q, spot] = t[bands:]


def contract(pieces, e0, e1, bands, first, count):
    slots = pieces[0].shape[0]
    return pl.pallas_call(
        functools.partial(contract_kernel, bands, slots, first, 8),
        out_shape=(kept((bands, slots, count, 3 * LANES)),) * 2,
        in_specs=[WHOLE] * (2 + len(pieces)),
        out_specs=[WHOLE] * 2,
        compiler_params=limit(8),
        name="contract",
    )(*in_vmem(e0, e1, *pieces))


def unpack_matrix(ref, k, s, size):
    half = size // 2
    j0, j1, j2 = (ref[k, pl.ds(2 * j + s, half, stride=6), :] for j in range(3))
    lane = lax.broadcasted_iota(jnp.int32, j0.shape, 1)
    r1 = pltpu.roll(j1, 64, 1)
    r2 = pltpu.roll(j2, 64, 1)
    return (j0, j1), (jnp.where(lane < 64, r1, r2), r2)


def join(a, b, size):
    return jnp.concatenate([a, b[:, 0 : size - LANES]], axis=1)


def prep_kernel(size, turn, spans, raw, hi, lo, buf, sem, left, right):
    half = size // 2
    count = raw.shape[0]
    copies = [
        pltpu.make_async_copy(raw.at[k], buf.at[k], sem.at[k]) for k in range(count)
    ]
    for c in copies:
        c.start()
    for k in range(count):
        copies[k].wait()
        mats = []
        for s in range(2):
            even, odd = unpack_matrix(buf, k, s, size)
            if turn:
                both = join(*even, size), join(*odd, size)
                rows = [x[a : a + n] for a, n in spans for x in both]
                turned = jnp.concatenate(rows, axis=0).T
                left[...] = turned[:, 0:LANES]
                right[:, 0 : size - LANES] = turned[:, LANES:size]
                rows = [
                    join(
                        left[pl.ds(p, half, stride=2), :],
                        right[pl.ds(p, half, stride=2), :],
                        size,
                    )
                    for p in range(2)
                ]
                mats.append(jnp.concatenate(rows, axis=0))
            else:
                for p, (a, b) in enumerate((even, odd)):
                    left[pl.ds(p, half, stride=2), :] = a
                    right[pl.ds(p, half, stride=2), :] = b
                mats.append(join(left[...], right[...], size))
        re, im = mats
        three = (re + im, re, im) if turn else (re, im - re, re + im)
        for i, m in enumerate(three):
            hi[k, i], lo[k, i] = split(m)


def prep(vectors, size, turn, spans):
    count, _, bb = vectors.shape
    tiles = bb // LANES
    view = vectors.reshape(count, 2, tiles, LANES).swapaxes(1, 2)
    view = view.reshape(count, 2 * tiles, LANES)
    return pl.pallas_call(
        functools.partial(prep_kernel, size, turn, spans),
        out_shape=(kept((count, 3, size, size), BF16),) * 2,
        in_specs=[RAW],
        out_specs=[WHOLE] * 2,
        scratch_shapes=[
            VMEM(view.shape, F32),
            pltpu.SemaphoreType.DMA((count,)),
            VMEM((size, LANES), F32),
            VMEM((size, LANES), F32),
        ],
        compiler_params=limit(8),
        name="prep",
    )(*in_hbm(view))


def angle_kernel(first, order, e0, e1, points, out):
    count, width = points.shape[1], len(order[0])
    row = lax.axis_index("row")
    lines = []
    for choice in zip(*order):
        if len(set(choice)) == 1:
            slot = choice[0]
        else:
            slot = sum(jnp.where(row == i, c, 0) for i, c in enumerate(choice))
        spot = pl.ds(first + slot, 1)
        lines.append(e0[spot, :] + e1[spot, :])
    lines = jnp.concatenate(lines, axis=0)
    cell = [jnp.broadcast_to(lines[:, d : d + 1], (width, LANES)) for d in range(4)]
    for k in range(count):
        turns = -cell[3]
        for d in range(3):
            turns = turns + cell[d] * points[d : d + 1, k : k + 1].astype(F32)
        turns = lax.rem(turns.astype(jnp.int32), G)
        turns = jnp.where(turns < 0, turns + G, turns)
        angle = turns.astype(F32) * (FULL_TURN / G)
        out[0, k * width : (k + 1) * width, :] = jnp.cos(angle)
        out[1, k * width : (k + 1) * width, :] = jnp.sin(angle)


def angles(e0, e1, points, first, order):
    lines = points.shape[0] * len(order[0])
    return pl.pallas_call(
        functools.partial(angle_kernel, first, order),
        out_shape=kept((2, lines, LANES)),
        in_specs=[WHOLE] * 3,
        out_specs=WHOLE,
        compiler_params=limit(4),
        name="angles",
    )(*in_vmem(e0, e1), points.T)


def rotated(refs, spec, cs, width, k, q0, group, re, im):
    for ref, (base, lines, slots) in zip(refs, spec):
        if not base <= q0 < base + lines:
            continue
        local = pl.ds(q0 - base, group)

        def turn(t, slot):
            spot = pl.ds(k * width + slot, 1)
            c, s = cs[0, spot, :], cs[1, spot, :]
            a, b = ref[t, 0, local, :], ref[t, 1, local, :]
            c, s = (jnp.concatenate([x] * 3, axis=1) for x in (c, s))
            return a * c - b * s, a * s + b * c

        if len(slots) <= 8:
            for t, slot in enumerate(slots):
                a, b = turn(t, slot)
                re = a if re is None else re + a
                im = b if im is None else im + b
        else:
            zero = jnp.zeros((group, 3 * LANES), F32)

            def step(t, carry):
                a, b = turn(t, t)
                return carry[0] + a, carry[1] + b

            start = (zero if re is None else re, zero if im is None else im)
            re, im = lax.fori_loop(0, len(slots), step, start)
    return re, im


def early_kernel(spec, width, group, *refs):
    blocks, cs, out = refs[: len(spec)], refs[-2], refs[-1]

    def one(k, carry):
        for q0 in range(0, out.shape[2], group):
            re, im = rotated(blocks, spec, cs, width, k, q0, group, None, None)
            out[k, 0, pl.ds(q0, group), :] = re
            out[k, 1, pl.ds(q0, group), :] = im
        return carry

    lax.fori_loop(0, out.shape[0], one, 0)


def early(blocks, spec, cs, count, half):
    width = cs.shape[1] // count
    return pl.pallas_call(
        functools.partial(early_kernel, spec, width, 8),
        out_shape=kept((count, 2, half, 3 * LANES)),
        in_specs=[WHOLE] * (len(blocks) + 1),
        out_specs=WHOLE,
        compiler_params=limit(4),
        name="early",
    )(*in_vmem(*blocks, cs))


def triple(xh, xl, yh, yl):
    rows = xh.shape[0]
    both = dot(jnp.concatenate([xh, xl], axis=0), yh)
    return both[0:rows] + both[rows:] + dot(xh, yl)


def load(span, width, spec, k, u, partial, blocks, cs, ph, plo):
    first, lines = span
    group = 16
    for q0 in range(first, first + lines, group):
        re, im = partial[k, 0, pl.ds(q0, group), :], partial[k, 1, pl.ds(q0, group), :]
        re, im = rotated(blocks, spec, cs, width, k, q0, group, re, im)
        for i, m in enumerate((re + im, re, im)):
            t0, t1, t2 = (m[:, j * LANES : (j + 1) * LANES] for j in range(3))
            for base, a, b in ((0, t0, t1), (lines, t2, pltpu.roll(t1, 64, 1))):
                spot = pl.ds(base + q0 - first, group)
                for dst, x, y in zip((ph, plo), split(a), split(b)):
                    dst[u, i, spot, 0:LANES] = x
                    dst[u, i, spot, LANES : 2 * LANES] = y


def product(size, k, u, ph, plo, wh, wl):
    k1, k2, k3 = (
        triple(ph[u, i][:, 0:size], plo[u, i][:, 0:size], wh[k, i], wl[k, i])
        for i in range(3)
    )
    return k1 - k3, k1 + k2


def inner_kernel(span, width, spec, size, unroll, partial, *refs):
    blocks = refs[: len(spec)]
    cs, wh, wl, out, ph, plo = refs[len(spec) :]
    first = pl.program_id(0) * unroll
    for u in range(unroll):
        load(span, width, spec, first + u, u, partial, blocks, cs, ph, plo)
    for u in range(unroll):
        k = first + u
        out[k, 0], out[k, 1] = product(size, k, u, ph, plo, wh, wl)


def halves(unroll, span):
    return [VMEM((unroll, 3, 2 * span[1], 2 * LANES), BF16)] * 2


def inner(span, partial, blocks, spec, cs, weights):
    count, _, size, _ = weights[0].shape
    unroll = 4 if count % 4 == 0 else 1
    return pl.pallas_call(
        functools.partial(inner_kernel, span, cs.shape[1] // count, spec, size, unroll),
        out_shape=kept((count, 2, 2 * span[1], size)),
        grid=(count // unroll,),
        in_specs=[WHOLE] * (4 + len(blocks)),
        out_specs=WHOLE,
        scratch_shapes=halves(unroll, span),
        compiler_params=limit(12),
        name="inner",
    )(*in_vmem(partial, *blocks, cs, *weights))


def final_kernel(span, width, spec, scale, size, unroll, done, partial, *refs):
    blocks = refs[: len(spec)]
    cs, gh, gl, wh, wl, out, ph, plo = refs[len(spec) :]
    half = size // 2
    first = pl.program_id(0) * unroll

    def outer(u, sums):
        k = first + u
        re, im = (jnp.concatenate([done[k, i], x], axis=0) for i, x in enumerate(sums))
        k1, k2, k3 = (
            triple(gh[k, i], gl[k, i], *split(m))
            for i, m in enumerate((re, im - re, re + im))
        )
        re, im = k1 - k3, k1 + k2
        return (re * re + im * im) * scale

    def store(u, value):
        tail = value[:, LANES:size]
        tail = jnp.concatenate([tail, tail], axis=1)
        turned = pltpu.roll(value[half:, 0:LANES], 64, 1)
        low = lax.broadcasted_iota(jnp.int32, turned.shape, 1) < 64
        out[u, pl.ds(0, half, stride=3), :] = value[0:half, 0:LANES]
        out[u, pl.ds(1, half, stride=3), :] = jnp.where(low, tail[0:half], turned)
        out[u, pl.ds(2, half, stride=3), :] = jnp.where(low, turned, tail[half:])

    for u in range(unroll):
        load(span, width, spec, first + u, u, partial, blocks, cs, ph, plo)
    sums = [product(size, first + u, u, ph, plo, wh, wl) for u in range(unroll)]
    for u in range(unroll):
        store(u, outer(u, sums[u]))


def final(span, done, partial, blocks, spec, cs, lefts, weights, total):
    count, _, size, _ = weights[0].shape
    tiles = size * size // LANES
    unroll = 4 if count % 4 == 0 else 1
    width = cs.shape[1] // count
    result = pl.pallas_call(
        functools.partial(final_kernel, span, width, spec, 1.0 / total, size, unroll),
        out_shape=jax.ShapeDtypeStruct((count, tiles, LANES), F32),
        grid=(count // unroll,),
        in_specs=[WHOLE] * (7 + len(blocks)),
        out_specs=pl.BlockSpec((unroll, tiles, LANES), lambda k: (k, 0, 0)),
        scratch_shapes=halves(unroll, span),
        compiler_params=limit(20),
        name="final",
    )(*in_vmem(done, partial, *blocks, cs, *lefts, *weights))
    return result.reshape(count, 1, size * size)


def swap(x, axis, bit, n):
    return lax.ppermute(x, axis, [(i, i ^ bit) for i in range(n)])


def edges(n):
    cycle = list(range(0, n, 2)) + list(range(n - 1, 0, -2))
    even, odd = [], []
    for i in range(0, n, 2):
        a, b, c = cycle[i], cycle[i + 1], cycle[(i + 2) % n]
        even += [(a, b), (b, a)]
        odd += [(b, c), (c, b)]
    return even, odd


def chunks(lines):
    return ((0, 2 * lines // 3), (2 * lines // 3, lines // 3))


def neighbour_gather(parts, n):
    even, odd = edges(n)
    moving = [p[None] for p in parts]
    held = [np.arange(n)[:, None] for _ in parts]
    blocks, sources = [[] for _ in parts], [[] for _ in parts]
    for step in range(n // 2):
        arrived = []
        for h in range(len(parts)):
            perm = (even, odd)[(step + h) % 2]
            arrived.append(lax.ppermute(moving[h], "row", perm))
            source = np.zeros_like(held[h])
            for a, b in perm:
                source[b] = held[h][a]
            if step == 0:
                source = np.concatenate([held[h], source], axis=1)
            held[h] = source
            sources[h].append(source)
        for h in range(len(parts)):
            if step == 0:
                arrived[h] = jnp.concatenate([moving[h], arrived[h]])
            moving[h] = arrived[h]
            blocks[h].append(moving[h])
    return blocks, [np.concatenate(s, axis=1) for s in sources]


def body(
    constants,
    current_modes,
    owner_id,
    live_count,
    triplets,
    center_point,
    pair_points,
    first_vectors,
    second_vectors,
):
    n_row, n_ba = lax.axis_size("row"), lax.axis_size("ba")
    slots, width, _ = constants.shape
    size = width * n_ba
    bands = current_modes.shape[-1]
    half = size // 2
    total = slots * n_row
    modes = jnp.swapaxes(current_modes[0], 1, 2)
    payload = pack(modes, owner_id, triplets, center_point, bands, slots, total)
    bit, hop = 1, 0
    while bit < n_row:
        if bit == FIRST and n_row >= 4 * bit:
            others = []
            for i in (1, 2, 3):
                others.append(swap(payload, "row", i * bit, n_row))
            bit *= 4
            payload = payload + others[0] + others[1] + others[2]
        else:
            other = swap(payload, "row", bit, n_row)
            bit *= 2
            if bit < n_row:
                payload = payload + other
        hop += 1
    cuts = 3 if width % 48 == 0 else 1
    pieces = []
    for i in range(cuts):
        pieces += fetch(constants, i * width // cuts, width // cuts)
    spans = chunks(half)
    weight = (jnp.arange(slots, dtype=jnp.int32) < live_count[0]).astype(F32)
    owns = []
    for base, lines in spans:
        keep, send = contract(pieces, payload, other, bands, base, lines)
        keep = keep.reshape(bands // 2, 2, slots, lines, 2 * size)
        send = send.reshape(bands // 2, 2, slots, lines, 2 * size)
        got = swap(send, "ba", 1, n_ba)
        far = swap(keep[1] + got[1], "ba", 2, n_ba)
        own = ((keep[0] + got[0]) + far) * weight[None, :, None, None]
        owns.append(own.swapaxes(0, 1))

    weights = prep(second_vectors, size, False, spans)
    lefts = prep(first_vectors, size, True, spans)
    if slots == 1 and n_row <= 8:
        parts, places = [], []
        for own, (base, lines) in zip(owns, spans):
            for start in (0, lines // 2):
                parts.append(own[0, :, start : start + lines // 2])
                places.append((base + start, lines // 2))
        blocks, sources = neighbour_gather(parts, n_row)
        order = np.concatenate(sources, axis=1)
        ahead, behind = [], [[] for _ in spans]
        for h, (base, lines) in enumerate(places):
            slot = h * n_row
            for n, b in enumerate(blocks[h]):
                here = range(slot, slot + b.shape[0])
                entry = (b, (base, lines, tuple(here)))
                (behind[h // 2] if n == len(blocks[h]) - 1 else ahead).append(entry)
                slot += b.shape[0]
    else:
        slots_all = tuple(range(total))
        ahead, behind = [], [[] for _ in spans]
        for own, (base, lines) in zip(owns, spans):
            gathered = lax.all_gather(own, "row", axis=0, tiled=True)
            ahead.append((gathered, (base, lines, slots_all)))
        order = np.broadcast_to(np.arange(total), (n_row, total))
    order = tuple(tuple(int(x) for x in line) for line in order)
    table = angles(payload, other, pair_points, 2 * bands, order)
    partial = early(*zip(*ahead), table, pair_points.shape[0], half)
    late = [tuple(zip(*b)) if b else ((), ()) for b in behind]
    done = inner(spans[0], partial, *late[0], table, weights)
    return final(spans[1], done, partial, *late[1], table, lefts, weights, total)


def solution(mesh):
    return jax.shard_map(
        body,
        mesh=mesh,
        in_specs=(
            P("row", "ba", None),
            P("row", None, "ba", None),
            P(),
            P("row"),
            P("row", None),
            P(),
            P("row", None),
            P("row", None, None),
            P("row", None, None),
        ),
        out_specs=P("row", "ba", None),
        check_vma=False,
    )
```

```python
import functools
import math

import jax
import jax.numpy as jnp
import numpy as np
from jax import lax
from jax.experimental import pallas as pl
from jax.experimental.pallas import tpu as pltpu
from jax.sharding import PartitionSpec as P

G = 32
UNROLL = 8
FIRST = 1
FULL_TURN = 2.0 * math.pi
LANES = 128
F32 = jnp.float32
BF16 = jnp.bfloat16
VMEM = pltpu.VMEM
SMEM = pltpu.SMEM


def split(x):
    hi = x.astype(BF16)
    lo = (x - hi.astype(F32)).astype(BF16)
    return hi, lo


def dot(a, b):
    return jnp.dot(a, b, preferred_element_type=F32)


def in_vmem(*xs):
    return [pltpu.with_memory_space_constraint(x, VMEM) for x in xs]


def in_hbm(*xs):
    return [pltpu.with_memory_space_constraint(x, pltpu.HBM) for x in xs]


def kept(shape, dtype=F32):
    return VMEM(shape, dtype)


WHOLE = pl.BlockSpec(memory_space=VMEM)
SCALARS = pl.BlockSpec(memory_space=SMEM)
RAW = pl.BlockSpec(memory_space=pltpu.HBM)


def limit(mib):
    return pltpu.CompilerParams(vmem_limit_bytes=mib << 20)


def pack_kernel(bands, slots, *refs):
    owner, raw, out, (trip, center, modes, sem) = refs[0], refs[1:4], refs[4], refs[5:]
    copies = [
        pltpu.make_async_copy(src, dst, sem.at[i])
        for i, (src, dst) in enumerate(zip(raw, (trip, center, modes)))
    ]
    for c in copies:
        c.start()
    out[...] = jnp.zeros_like(out)
    for c in copies:
        c.wait()
    row, ba = lax.axis_index("row"), lax.axis_index("ba")
    mine = (owner[0] == row).astype(F32)
    width = modes.shape[-1]
    order = [j for j in range(bands) if j % 2 == 0] + [j for j in range(bands) if j % 2]
    for place, j in enumerate(order):
        for s in range(2):
            line = modes[s, pl.ds(lax.bitwise_xor(ba, j), 1), :]
            out[pl.ds(place * 2 + s, 1), 0:width] = line * mine
    lane = lax.broadcasted_iota(jnp.int32, (1, LANES), 1)
    for r in range(slots):
        shift = 0
        entry = jnp.zeros((1, LANES), jnp.int32)
        for d in range(3):
            entry = jnp.where(lane == d, trip[r, d] - trip[r, 3 + d], entry)
            shift = shift + trip[r, 3 + d] * center[d]
        entry = jnp.where(lane == 3, shift, entry)
        out[pl.ds(2 * bands + row * slots + r, 1), :] = entry.astype(F32)


def pack(modes, owner, trip, center, bands, slots, total):
    rows = 2 * bands + -(-total // 8) * 8
    return pl.pallas_call(
        functools.partial(pack_kernel, bands, slots),
        out_shape=kept((rows, LANES)),
        in_specs=[SCALARS] + [RAW] * 3,
        out_specs=WHOLE,
        scratch_shapes=[SMEM(x.shape, x.dtype) for x in (trip, center)]
        + [VMEM(modes.shape, F32), pltpu.SemaphoreType.DMA((3,))],
        compiler_params=limit(4),
        name="pack",
    )(owner, *in_hbm(trip, center, modes))


def fetch_kernel(slots, first, rows, parts, const, hi, lo, buf, sem):
    width = const.shape[2] // parts
    copies = []
    for r in range(slots):
        for i in range(parts):
            lanes = pl.ds(i * width, width)
            copies.append(
                pltpu.make_async_copy(
                    const.at[r, pl.ds(first, rows), lanes], buf.at[r, :, lanes], sem.at[r, i]
                )
            )
    for c in copies:
        c.start()
    for n, c in enumerate(copies):
        c.wait()
        r, i = n // parts, n % parts
        lanes = slice(i * width, (i + 1) * width)
        hi[r, :, lanes], lo[r, :, lanes] = split(buf[r, :, lanes])


def fetch(constants, first, rows):
    slots, _, bb = constants.shape
    parts = 6
    return pl.pallas_call(
        functools.partial(fetch_kernel, slots, first, rows, parts),
        out_shape=(kept((slots, rows, bb), BF16),) * 2,
        in_specs=[RAW],
        out_specs=[WHOLE] * 2,
        scratch_shapes=[
            VMEM((slots, rows, bb), F32),
            pltpu.SemaphoreType.DMA((slots, parts)),
        ],
        compiler_params=limit(8),
        name="fetch",
    )(*in_hbm(constants))


def contract_kernel(bands, slots, first, lines, e0, e1, *refs):
    pieces, (keep, send) = refs[:-2], refs[-2:]
    his, los = pieces[0::2], pieces[1::2]
    width = sum(h.shape[1] for h in his)
    total = e0[...] + e1[...]
    eigen = total[0 : 2 * bands, 0:width]
    pairs, chunk = keep.shape[2], keep.shape[3]
    low = lax.broadcasted_iota(jnp.int32, (2 * bands, LANES), 1) < 64
    for r in range(slots):
        eh, el = split(eigen)
        left = jnp.concatenate(
            [
                jnp.concatenate([eh, eh], axis=1),
                jnp.concatenate([el, jnp.zeros_like(el)], axis=1),
            ],
            axis=0,
        )
        for base in range(0, pairs, lines):
            lanes = slice((first + base) * chunk, (first + base + lines) * chunk)
            right = jnp.concatenate(
                [h[r, :, lanes] for h in his] + [m[r, :, lanes] for m in los], axis=0
            )
            both = dot(left, right)
            res = both[0 : 2 * bands] + both[2 * bands :]
            for q in range(lines):
                j0, j1, j2 = (
                    res[:, q * chunk + j * LANES : q * chunk + (j + 1) * LANES]
                    for j in range(3)
                )
                t1 = jnp.where(low, j1, j2)
                t2 = jnp.where(low, pltpu.roll(j1, 64, 1), pltpu.roll(j2, 64, 1))
                for j, t in enumerate((j0, t1, t2)):
                    spot = slice(j * LANES, (j + 1) * LANES)
                    keep[:, r, base + q, spot] = t[0:bands]
                    send[:, r, base + q, spot] = t[bands:]


def contract(pieces, e0, e1, bands, first, count):
    slots = pieces[0].shape[0]
    return pl.pallas_call(
        functools.partial(contract_kernel, bands, slots, first, 8),
        out_shape=(kept((bands, slots, count, 3 * LANES)),) * 2,
        in_specs=[WHOLE] * (2 + len(pieces)),
        out_specs=[WHOLE] * 2,
        compiler_params=limit(8),
        name="contract",
    )(*in_vmem(e0, e1, *pieces))


def unpack_matrix(ref, k, s, size):
    half = size // 2
    j0, j1, j2 = (ref[k, pl.ds(2 * j + s, half, stride=6), :] for j in range(3))
    lane = lax.broadcasted_iota(jnp.int32, j0.shape, 1)
    r1 = pltpu.roll(j1, 64, 1)
    r2 = pltpu.roll(j2, 64, 1)
    return (j0, j1), (jnp.where(lane < 64, r1, r2), r2)


def join(a, b, size):
    return jnp.concatenate([a, b[:, 0 : size - LANES]], axis=1)


def prep_kernel(size, turn, spans, raw, hi, lo, buf, sem, left, right):
    half = size // 2
    count = raw.shape[0]
    copies = [
        pltpu.make_async_copy(raw.at[k], buf.at[k], sem.at[k]) for k in range(count)
    ]
    for c in copies:
        c.start()
    for k in range(count):
        copies[k].wait()
        mats = []
        for s in range(2):
            even, odd = unpack_matrix(buf, k, s, size)
            if turn:
                both = join(*even, size), join(*odd, size)
                rows = [x[a : a + n] for a, n in spans for x in both]
                turned = jnp.concatenate(rows, axis=0).T
                left[...] = turned[:, 0:LANES]
                right[:, 0 : size - LANES] = turned[:, LANES:size]
                rows = [
                    join(
                        left[pl.ds(p, half, stride=2), :],
                        right[pl.ds(p, half, stride=2), :],
                        size,
                    )
                    for p in range(2)
                ]
                mats.append(jnp.concatenate(rows, axis=0))
            else:
                for p, (a, b) in enumerate((even, odd)):
                    left[pl.ds(p, half, stride=2), :] = a
                    right[pl.ds(p, half, stride=2), :] = b
                mats.append(join(left[...], right[...], size))
        re, im = mats
        three = (re + im, re, im) if turn else (re, im - re, re + im)
        for i, m in enumerate(three):
            hi[k, i], lo[k, i] = split(m)


def prep(vectors, size, turn, spans):
    count, _, bb = vectors.shape
    tiles = bb // LANES
    view = vectors.reshape(count, 2, tiles, LANES).swapaxes(1, 2)
    view = view.reshape(count, 2 * tiles, LANES)
    return pl.pallas_call(
        functools.partial(prep_kernel, size, turn, spans),
        out_shape=(kept((count, 3, size, size), BF16),) * 2,
        in_specs=[RAW],
        out_specs=[WHOLE] * 2,
        scratch_shapes=[
            VMEM(view.shape, F32),
            pltpu.SemaphoreType.DMA((count,)),
            VMEM((size, LANES), F32),
            VMEM((size, LANES), F32),
        ],
        compiler_params=limit(8),
        name="prep",
    )(*in_hbm(view))


def angle_kernel(first, order, e0, e1, points, out):
    count, width = points.shape[1], len(order[0])
    row = lax.axis_index("row")
    lines = []
    for choice in zip(*order):
        if len(set(choice)) == 1:
            slot = choice[0]
        else:
            slot = sum(jnp.where(row == i, c, 0) for i, c in enumerate(choice))
        spot = pl.ds(first + slot, 1)
        lines.append(e0[spot, :] + e1[spot, :])
    lines = jnp.concatenate(lines, axis=0)
    cell = [jnp.broadcast_to(lines[:, d : d + 1], (width, LANES)) for d in range(4)]
    for k in range(count):
        turns = -cell[3]
        for d in range(3):
            turns = turns + cell[d] * points[d : d + 1, k : k + 1].astype(F32)
        turns = lax.rem(turns.astype(jnp.int32), G)
        turns = jnp.where(turns < 0, turns + G, turns)
        angle = turns.astype(F32) * (FULL_TURN / G)
        out[0, k * width : (k + 1) * width, :] = jnp.cos(angle)
        out[1, k * width : (k + 1) * width, :] = jnp.sin(angle)


def angles(e0, e1, points, first, order):
    lines = points.shape[0] * len(order[0])
    return pl.pallas_call(
        functools.partial(angle_kernel, first, order),
        out_shape=kept((2, lines, LANES)),
        in_specs=[WHOLE] * 3,
        out_specs=WHOLE,
        compiler_params=limit(4),
        name="angles",
    )(*in_vmem(e0, e1), points.T)


def rotated(refs, spec, cs, width, k, q0, group, re, im):
    for ref, (base, lines, slots) in zip(refs, spec):
        if not base <= q0 < base + lines:
            continue
        local = pl.ds(q0 - base, group)

        def turn(t, slot):
            spot = pl.ds(k * width + slot, 1)
            c, s = cs[0, spot, :], cs[1, spot, :]
            a, b = ref[t, 0, local, :], ref[t, 1, local, :]
            c, s = (jnp.concatenate([x] * 3, axis=1) for x in (c, s))
            return a * c - b * s, a * s + b * c

        if len(slots) <= 8:
            for t, slot in enumerate(slots):
                a, b = turn(t, slot)
                re = a if re is None else re + a
                im = b if im is None else im + b
        else:
            zero = jnp.zeros((group, 3 * LANES), F32)

            def step(t, carry):
                a, b = turn(t, t)
                return carry[0] + a, carry[1] + b

            start = (zero if re is None else re, zero if im is None else im)
            re, im = lax.fori_loop(0, len(slots), step, start)
    return re, im


def early_kernel(spec, width, group, *refs):
    blocks, cs, out = refs[: len(spec)], refs[-2], refs[-1]

    def one(k, carry):
        for q0 in range(0, out.shape[2], group):
            re, im = rotated(blocks, spec, cs, width, k, q0, group, None, None)
            out[k, 0, pl.ds(q0, group), :] = re
            out[k, 1, pl.ds(q0, group), :] = im
        return carry

    lax.fori_loop(0, out.shape[0], one, 0)


def early(blocks, spec, cs, count, half):
    width = cs.shape[1] // count
    return pl.pallas_call(
        functools.partial(early_kernel, spec, width, 8),
        out_shape=kept((count, 2, half, 3 * LANES)),
        in_specs=[WHOLE] * (len(blocks) + 1),
        out_specs=WHOLE,
        compiler_params=limit(4),
        name="early",
    )(*in_vmem(*blocks, cs))


def triple(xh, xl, yh, yl):
    rows = xh.shape[0]
    both = dot(jnp.concatenate([xh, xl], axis=0), yh)
    return both[0:rows] + both[rows:] + dot(xh, yl)


def load(span, width, spec, k, u, partial, blocks, cs, ph, plo):
    first, lines = span
    group = 16
    for q0 in range(first, first + lines, group):
        re, im = partial[k, 0, pl.ds(q0, group), :], partial[k, 1, pl.ds(q0, group), :]
        re, im = rotated(blocks, spec, cs, width, k, q0, group, re, im)
        for i, m in enumerate((re + im, re, im)):
            t0, t1, t2 = (m[:, j * LANES : (j + 1) * LANES] for j in range(3))
            for base, a, b in ((0, t0, t1), (lines, t2, pltpu.roll(t1, 64, 1))):
                spot = pl.ds(base + q0 - first, group)
                for dst, x, y in zip((ph, plo), split(a), split(b)):
                    dst[u, i, spot, 0:LANES] = x
                    dst[u, i, spot, LANES : 2 * LANES] = y


def product(size, k, u, ph, plo, wh, wl):
    k1, k2, k3 = (
        triple(ph[u, i][:, 0:size], plo[u, i][:, 0:size], wh[k, i], wl[k, i])
        for i in range(3)
    )
    return k1 - k3, k1 + k2


def inner_kernel(span, width, spec, size, unroll, partial, *refs):
    blocks = refs[: len(spec)]
    cs, wh, wl, out, ph, plo = refs[len(spec) :]
    first = pl.program_id(0) * unroll
    for u in range(unroll):
        load(span, width, spec, first + u, u, partial, blocks, cs, ph, plo)
    for u in range(unroll):
        k = first + u
        out[k, 0], out[k, 1] = product(size, k, u, ph, plo, wh, wl)


def halves(unroll, span):
    return [VMEM((unroll, 3, 2 * span[1], 2 * LANES), BF16)] * 2


def inner(span, partial, blocks, spec, cs, weights):
    count, _, size, _ = weights[0].shape
    unroll = UNROLL
    while count % unroll:
        unroll //= 2
    return pl.pallas_call(
        functools.partial(inner_kernel, span, cs.shape[1] // count, spec, size, unroll),
        out_shape=kept((count, 2, 2 * span[1], size)),
        grid=(count // unroll,),
        in_specs=[WHOLE] * (4 + len(blocks)),
        out_specs=WHOLE,
        scratch_shapes=halves(unroll, span),
        compiler_params=limit(12),
        name="inner",
    )(*in_vmem(partial, *blocks, cs, *weights))


def final_kernel(span, width, spec, scale, size, unroll, done, partial, *refs):
    blocks = refs[: len(spec)]
    cs, gh, gl, wh, wl, raw, ph, plo, out, sem = refs[len(spec) :]
    half = size // 2
    first = pl.program_id(0) * unroll

    def outer(u, sums):
        k = first + u
        re, im = (jnp.concatenate([done[k, i], x], axis=0) for i, x in enumerate(sums))
        k1, k2, k3 = (
            triple(gh[k, i], gl[k, i], *split(m))
            for i, m in enumerate((re, im - re, re + im))
        )
        re, im = k1 - k3, k1 + k2
        return (re * re + im * im) * scale

    def store(u, value):
        tail = value[:, LANES:size]
        tail = jnp.concatenate([tail, tail], axis=1)
        turned = pltpu.roll(value[half:, 0:LANES], 64, 1)
        low = lax.broadcasted_iota(jnp.int32, turned.shape, 1) < 64
        out[u, pl.ds(0, half, stride=3), :] = value[0:half, 0:LANES]
        out[u, pl.ds(1, half, stride=3), :] = jnp.where(low, tail[0:half], turned)
        out[u, pl.ds(2, half, stride=3), :] = jnp.where(low, turned, tail[half:])

    for u in range(unroll):
        load(span, width, spec, first + u, u, partial, blocks, cs, ph, plo)
    sums = [product(size, first + u, u, ph, plo, wh, wl) for u in range(2)]
    copies = []
    for u in range(unroll):
        if u + 2 < unroll:
            sums.append(product(size, first + u + 2, u + 2, ph, plo, wh, wl))
        store(u, outer(u, sums[u]))
        copies.append(pltpu.make_async_copy(out.at[u], raw.at[first + u], sem.at[u]))
        copies[-1].start()
    for c in copies:
        c.wait()


def final(span, done, partial, blocks, spec, cs, lefts, weights, total):
    count, _, size, _ = weights[0].shape
    tiles = size * size // LANES
    unroll = UNROLL
    while count % unroll:
        unroll //= 2
    width = cs.shape[1] // count
    result = pl.pallas_call(
        functools.partial(final_kernel, span, width, spec, 1.0 / total, size, unroll),
        out_shape=jax.ShapeDtypeStruct((count, tiles, LANES), F32),
        grid=(count // unroll,),
        in_specs=[WHOLE] * (7 + len(blocks)),
        out_specs=RAW,
        scratch_shapes=halves(unroll, span)
        + [VMEM((unroll, tiles, LANES), F32), pltpu.SemaphoreType.DMA((unroll,))],
        compiler_params=limit(24),
        name="final",
    )(*in_vmem(done, partial, *blocks, cs, *lefts, *weights))
    return result.reshape(count, 1, size * size)


def swap(x, axis, bit, n):
    return lax.ppermute(x, axis, [(i, i ^ bit) for i in range(n)])


def edges(n):
    cycle = list(range(0, n, 2)) + list(range(n - 1, 0, -2))
    even, odd = [], []
    for i in range(0, n, 2):
        a, b, c = cycle[i], cycle[i + 1], cycle[(i + 2) % n]
        even += [(a, b), (b, a)]
        odd += [(b, c), (c, b)]
    return even, odd


def chunks(lines):
    return ((0, 2 * lines // 3), (2 * lines // 3, lines // 3))


def neighbour_gather(parts, n):
    even, odd = edges(n)
    moving = [p[None] for p in parts]
    held = [np.arange(n)[:, None] for _ in parts]
    blocks, sources = [[] for _ in parts], [[] for _ in parts]
    for step in range(n // 2):
        arrived = []
        for h in range(len(parts)):
            perm = (even, odd)[(step + h) % 2]
            arrived.append(lax.ppermute(moving[h], "row", perm))
            source = np.zeros_like(held[h])
            for a, b in perm:
                source[b] = held[h][a]
            if step == 0:
                source = np.concatenate([held[h], source], axis=1)
            held[h] = source
            sources[h].append(source)
        for h in range(len(parts)):
            if step == 0:
                arrived[h] = jnp.concatenate([moving[h], arrived[h]])
            moving[h] = arrived[h]
            blocks[h].append(moving[h])
    return blocks, [np.concatenate(s, axis=1) for s in sources]


def body(
    constants,
    current_modes,
    owner_id,
    live_count,
    triplets,
    center_point,
    pair_points,
    first_vectors,
    second_vectors,
):
    n_row, n_ba = lax.axis_size("row"), lax.axis_size("ba")
    slots, width, _ = constants.shape
    size = width * n_ba
    bands = current_modes.shape[-1]
    half = size // 2
    total = slots * n_row
    modes = jnp.swapaxes(current_modes[0], 1, 2)
    payload = pack(modes, owner_id, triplets, center_point, bands, slots, total)
    bit, hop = 1, 0
    while bit < n_row:
        if bit == FIRST and n_row >= 4 * bit:
            others = []
            for i in (1, 2, 3):
                others.append(swap(payload, "row", i * bit, n_row))
            bit *= 4
            payload = payload + others[0] + others[1] + others[2]
        else:
            other = swap(payload, "row", bit, n_row)
            bit *= 2
            if bit < n_row:
                payload = payload + other
        hop += 1
    cuts = 3 if width % 48 == 0 else 1
    pieces = []
    for i in range(cuts):
        pieces += fetch(constants, i * width // cuts, width // cuts)
    spans = chunks(half)
    weight = (jnp.arange(slots, dtype=jnp.int32) < live_count[0]).astype(F32)
    owns = []
    for base, lines in spans:
        keep, send = contract(pieces, payload, other, bands, base, lines)
        keep = keep.reshape(bands // 2, 2, slots, lines, 2 * size)
        send = send.reshape(bands // 2, 2, slots, lines, 2 * size)
        got = swap(send, "ba", 1, n_ba)
        far = swap(keep[1] + got[1], "ba", 2, n_ba)
        own = ((keep[0] + got[0]) + far) * weight[None, :, None, None]
        owns.append(own.swapaxes(0, 1))

    weights = prep(second_vectors, size, False, spans)
    lefts = prep(first_vectors, size, True, spans)
    if slots == 1 and n_row <= 8:
        parts, places = [], []
        for own, (base, lines) in zip(owns, spans):
            for start in (0, lines // 2):
                parts.append(own[0, :, start : start + lines // 2])
                places.append((base + start, lines // 2))
        blocks, sources = neighbour_gather(parts, n_row)
        order = np.concatenate(sources, axis=1)
        ahead, behind = [], [[] for _ in spans]
        for h, (base, lines) in enumerate(places):
            slot = h * n_row
            for n, b in enumerate(blocks[h]):
                here = range(slot, slot + b.shape[0])
                entry = (b, (base, lines, tuple(here)))
                (behind[h // 2] if n == len(blocks[h]) - 1 else ahead).append(entry)
                slot += b.shape[0]
    else:
        slots_all = tuple(range(total))
        ahead, behind = [], [[] for _ in spans]
        for own, (base, lines) in zip(owns, spans):
            gathered = lax.all_gather(own, "row", axis=0, tiled=True)
            ahead.append((gathered, (base, lines, slots_all)))
        order = np.broadcast_to(np.arange(total), (n_row, total))
    order = tuple(tuple(int(x) for x in line) for line in order)
    table = angles(payload, other, pair_points, 2 * bands, order)
    partial = early(*zip(*ahead), table, pair_points.shape[0], half)
    late = [tuple(zip(*b)) if b else ((), ()) for b in behind]
    done = inner(spans[0], partial, *late[0], table, weights)
    return final(spans[1], done, partial, *late[1], table, lefts, weights, total)


def solution(mesh):
    return jax.shard_map(
        body,
        mesh=mesh,
        in_specs=(
            P("row", "ba", None),
            P("row", None, "ba", None),
            P(),
            P("row"),
            P("row", None),
            P(),
            P("row", None),
            P("row", None, None),
            P("row", None, None),
        ),
        out_specs=P("row", "ba", None),
        check_vma=False,
    )
```

```python
import functools
import math

import jax
import jax.numpy as jnp
import numpy as np
from jax import lax
from jax.experimental import pallas as pl
from jax.experimental.pallas import tpu as pltpu
from jax.sharding import PartitionSpec as P

G = 32
UNROLL = 8
FIRST = 1
FULL_TURN = 2.0 * math.pi
LANES = 128
F32 = jnp.float32
BF16 = jnp.bfloat16
VMEM = pltpu.VMEM
SMEM = pltpu.SMEM


def split(x):
    hi = x.astype(BF16)
    lo = (x - hi.astype(F32)).astype(BF16)
    return hi, lo


def dot(a, b):
    return jnp.dot(a, b, preferred_element_type=F32)


def in_vmem(*xs):
    return [pltpu.with_memory_space_constraint(x, VMEM) for x in xs]


def in_hbm(*xs):
    return [pltpu.with_memory_space_constraint(x, pltpu.HBM) for x in xs]


def kept(shape, dtype=F32):
    return VMEM(shape, dtype)


WHOLE = pl.BlockSpec(memory_space=VMEM)
SCALARS = pl.BlockSpec(memory_space=SMEM)
RAW = pl.BlockSpec(memory_space=pltpu.HBM)


def limit(mib):
    return pltpu.CompilerParams(vmem_limit_bytes=mib << 20)


def pack_kernel(bands, slots, *refs):
    owner, raw, out, (trip, center, modes, sem) = refs[0], refs[1:4], refs[4], refs[5:]
    copies = [
        pltpu.make_async_copy(src, dst, sem.at[i])
        for i, (src, dst) in enumerate(zip(raw, (trip, center, modes)))
    ]
    for c in copies:
        c.start()
    out[...] = jnp.zeros_like(out)
    for c in copies:
        c.wait()
    row, ba = lax.axis_index("row"), lax.axis_index("ba")
    mine = (owner[0] == row).astype(F32)
    width = modes.shape[-1]
    order = [j for j in range(bands) if j % 2 == 0] + [j for j in range(bands) if j % 2]
    for place, j in enumerate(order):
        for s in range(2):
            line = modes[s, pl.ds(lax.bitwise_xor(ba, j), 1), :]
            out[pl.ds(place * 2 + s, 1), 0:width] = line * mine
    lane = lax.broadcasted_iota(jnp.int32, (1, LANES), 1)
    for r in range(slots):
        shift = 0
        entry = jnp.zeros((1, LANES), jnp.int32)
        for d in range(3):
            entry = jnp.where(lane == d, trip[r, d] - trip[r, 3 + d], entry)
            shift = shift + trip[r, 3 + d] * center[d]
        entry = jnp.where(lane == 3, shift, entry)
        out[pl.ds(2 * bands + row * slots + r, 1), :] = entry.astype(F32)


def pack(modes, owner, trip, center, bands, slots, total):
    rows = 2 * bands + -(-total // 8) * 8
    return pl.pallas_call(
        functools.partial(pack_kernel, bands, slots),
        out_shape=kept((rows, LANES)),
        in_specs=[SCALARS] + [RAW] * 3,
        out_specs=WHOLE,
        scratch_shapes=[SMEM(x.shape, x.dtype) for x in (trip, center)]
        + [VMEM(modes.shape, F32), pltpu.SemaphoreType.DMA((3,))],
        compiler_params=limit(4),
        name="pack",
    )(owner, *in_hbm(trip, center, modes))


def fetch_kernel(slots, first, rows, parts, const, hi, lo, buf, sem):
    width = const.shape[2] // parts
    copies = []
    for r in range(slots):
        for i in range(parts):
            lanes = pl.ds(i * width, width)
            copies.append(
                pltpu.make_async_copy(
                    const.at[r, pl.ds(first, rows), lanes], buf.at[r, :, lanes], sem.at[r, i]
                )
            )
    for c in copies:
        c.start()
    for n, c in enumerate(copies):
        c.wait()
        r, i = n // parts, n % parts
        lanes = slice(i * width, (i + 1) * width)
        hi[r, :, lanes], lo[r, :, lanes] = split(buf[r, :, lanes])


def fetch(constants, first, rows):
    slots, _, bb = constants.shape
    parts = 6
    return pl.pallas_call(
        functools.partial(fetch_kernel, slots, first, rows, parts),
        out_shape=(kept((slots, rows, bb), BF16),) * 2,
        in_specs=[RAW],
        out_specs=[WHOLE] * 2,
        scratch_shapes=[
            VMEM((slots, rows, bb), F32),
            pltpu.SemaphoreType.DMA((slots, parts)),
        ],
        compiler_params=limit(8),
        name="fetch",
    )(*in_hbm(constants))


def contract_kernel(bands, slots, first, lines, e0, e1, *refs):
    pieces, (keep, send) = refs[:-2], refs[-2:]
    his, los = pieces[0::2], pieces[1::2]
    width = sum(h.shape[1] for h in his)
    total = e0[...] + e1[...]
    eigen = total[0 : 2 * bands, 0:width]
    pairs, chunk = keep.shape[2], keep.shape[3]
    low = lax.broadcasted_iota(jnp.int32, (2 * bands, LANES), 1) < 64
    for r in range(slots):
        eh, el = split(eigen)
        left = jnp.concatenate(
            [
                jnp.concatenate([eh, eh], axis=1),
                jnp.concatenate([el, jnp.zeros_like(el)], axis=1),
            ],
            axis=0,
        )
        for base in range(0, pairs, lines):
            lanes = slice((first + base) * chunk, (first + base + lines) * chunk)
            right = jnp.concatenate(
                [h[r, :, lanes] for h in his] + [m[r, :, lanes] for m in los], axis=0
            )
            both = dot(left, right)
            res = both[0 : 2 * bands] + both[2 * bands :]
            for q in range(lines):
                j0, j1, j2 = (
                    res[:, q * chunk + j * LANES : q * chunk + (j + 1) * LANES]
                    for j in range(3)
                )
                t1 = jnp.where(low, j1, j2)
                t2 = jnp.where(low, pltpu.roll(j1, 64, 1), pltpu.roll(j2, 64, 1))
                for j, t in enumerate((j0, t1, t2)):
                    spot = slice(j * LANES, (j + 1) * LANES)
                    keep[:, r, base + q, spot] = t[0:bands]
                    send[:, r, base + q, spot] = t[bands:]


def contract(pieces, e0, e1, bands, first, count):
    slots = pieces[0].shape[0]
    return pl.pallas_call(
        functools.partial(contract_kernel, bands, slots, first, 8),
        out_shape=(kept((bands, slots, count, 3 * LANES)),) * 2,
        in_specs=[WHOLE] * (2 + len(pieces)),
        out_specs=[WHOLE] * 2,
        compiler_params=limit(8),
        name="contract",
    )(*in_vmem(e0, e1, *pieces))


def unpack_matrix(ref, k, s, size):
    half = size // 2
    j0, j1, j2 = (ref[k, pl.ds(2 * j + s, half, stride=6), :] for j in range(3))
    lane = lax.broadcasted_iota(jnp.int32, j0.shape, 1)
    r1 = pltpu.roll(j1, 64, 1)
    r2 = pltpu.roll(j2, 64, 1)
    return (j0, j1), (jnp.where(lane < 64, r1, r2), r2)


def join(a, b, size):
    return jnp.concatenate([a, b[:, 0 : size - LANES]], axis=1)


def prep_kernel(size, turn, spans, raw, hi, lo, buf, sem, left, right):
    half = size // 2
    count = raw.shape[0]
    copies = [
        pltpu.make_async_copy(raw.at[k], buf.at[k], sem.at[k]) for k in range(count)
    ]
    for c in copies:
        c.start()
    for k in range(count):
        copies[k].wait()
        mats = []
        for s in range(2):
            even, odd = unpack_matrix(buf, k, s, size)
            if turn:
                both = join(*even, size), join(*odd, size)
                rows = [x[a : a + n] for a, n in spans for x in both]
                turned = jnp.concatenate(rows, axis=0).T
                left[...] = turned[:, 0:LANES]
                right[:, 0 : size - LANES] = turned[:, LANES:size]
                rows = [
                    join(
                        left[pl.ds(p, half, stride=2), :],
                        right[pl.ds(p, half, stride=2), :],
                        size,
                    )
                    for p in range(2)
                ]
                mats.append(jnp.concatenate(rows, axis=0))
            else:
                for p, (a, b) in enumerate((even, odd)):
                    left[pl.ds(p, half, stride=2), :] = a
                    right[pl.ds(p, half, stride=2), :] = b
                mats.append(join(left[...], right[...], size))
        re, im = mats
        three = (re + im, re, im) if turn else (re, im - re, re + im)
        for i, m in enumerate(three):
            hi[k, i], lo[k, i] = split(m)


def prep(vectors, size, turn, spans):
    count, _, bb = vectors.shape
    tiles = bb // LANES
    view = vectors.reshape(count, 2, tiles, LANES).swapaxes(1, 2)
    view = view.reshape(count, 2 * tiles, LANES)
    return pl.pallas_call(
        functools.partial(prep_kernel, size, turn, spans),
        out_shape=(kept((count, 3, size, size), BF16),) * 2,
        in_specs=[RAW],
        out_specs=[WHOLE] * 2,
        scratch_shapes=[
            VMEM(view.shape, F32),
            pltpu.SemaphoreType.DMA((count,)),
            VMEM((size, LANES), F32),
            VMEM((size, LANES), F32),
        ],
        compiler_params=limit(8),
        name="prep",
    )(*in_hbm(view))


def angle_kernel(first, order, e0, e1, points, out):
    count, width = points.shape[1], len(order[0])
    row = lax.axis_index("row")
    lines = []
    for choice in zip(*order):
        if len(set(choice)) == 1:
            slot = choice[0]
        else:
            slot = sum(jnp.where(row == i, c, 0) for i, c in enumerate(choice))
        spot = pl.ds(first + slot, 1)
        lines.append(e0[spot, :] + e1[spot, :])
    lines = jnp.concatenate(lines, axis=0)
    cell = [jnp.broadcast_to(lines[:, d : d + 1], (width, LANES)) for d in range(4)]
    for k in range(count):
        turns = -cell[3]
        for d in range(3):
            turns = turns + cell[d] * points[d : d + 1, k : k + 1].astype(F32)
        turns = lax.rem(turns.astype(jnp.int32), G)
        turns = jnp.where(turns < 0, turns + G, turns)
        angle = turns.astype(F32) * (FULL_TURN / G)
        out[0, k * width : (k + 1) * width, :] = jnp.cos(angle)
        out[1, k * width : (k + 1) * width, :] = jnp.sin(angle)


def angles(e0, e1, points, first, order):
    lines = points.shape[0] * len(order[0])
    return pl.pallas_call(
        functools.partial(angle_kernel, first, order),
        out_shape=kept((2, lines, LANES)),
        in_specs=[WHOLE] * 3,
        out_specs=WHOLE,
        compiler_params=limit(4),
        name="angles",
    )(*in_vmem(e0, e1), points.T)


def rotated(refs, spec, cs, width, k, q0, group, re, im):
    for ref, (base, lines, slots) in zip(refs, spec):
        if not base <= q0 < base + lines:
            continue
        local = pl.ds(q0 - base, group)

        def turn(t, slot):
            spot = pl.ds(k * width + slot, 1)
            c, s = cs[0, spot, :], cs[1, spot, :]
            a, b = ref[t, 0, local, :], ref[t, 1, local, :]
            c, s = (jnp.concatenate([x] * 3, axis=1) for x in (c, s))
            return a * c - b * s, a * s + b * c

        if len(slots) <= 8:
            for t, slot in enumerate(slots):
                a, b = turn(t, slot)
                re = a if re is None else re + a
                im = b if im is None else im + b
        else:
            zero = jnp.zeros((group, 3 * LANES), F32)

            def step(t, carry):
                a, b = turn(t, t)
                return carry[0] + a, carry[1] + b

            start = (zero if re is None else re, zero if im is None else im)
            re, im = lax.fori_loop(0, len(slots), step, start)
    return re, im


def early_kernel(spec, width, group, *refs):
    blocks, cs, out = refs[: len(spec)], refs[-2], refs[-1]

    def one(k, carry):
        for q0 in range(0, out.shape[2], group):
            re, im = rotated(blocks, spec, cs, width, k, q0, group, None, None)
            out[k, 0, pl.ds(q0, group), :] = re
            out[k, 1, pl.ds(q0, group), :] = im
        return carry

    lax.fori_loop(0, out.shape[0], one, 0)


def early(blocks, spec, cs, count, half):
    width = cs.shape[1] // count
    return pl.pallas_call(
        functools.partial(early_kernel, spec, width, 8),
        out_shape=kept((count, 2, half, 3 * LANES)),
        in_specs=[WHOLE] * (len(blocks) + 1),
        out_specs=WHOLE,
        compiler_params=limit(4),
        name="early",
    )(*in_vmem(*blocks, cs))


def triple(xh, xl, yh, yl):
    rows = xh.shape[0]
    both = dot(jnp.concatenate([xh, xl], axis=0), yh)
    return both[0:rows] + both[rows:] + dot(xh, yl)


def load(span, width, spec, k, u, partial, blocks, cs, ph, plo):
    first, lines = span
    group = 16
    for q0 in range(first, first + lines, group):
        re, im = partial[k, 0, pl.ds(q0, group), :], partial[k, 1, pl.ds(q0, group), :]
        re, im = rotated(blocks, spec, cs, width, k, q0, group, re, im)
        for i, m in enumerate((re + im, re, im)):
            t0, t1, t2 = (m[:, j * LANES : (j + 1) * LANES] for j in range(3))
            for base, a, b in ((0, t0, t1), (lines, t2, pltpu.roll(t1, 64, 1))):
                spot = pl.ds(base + q0 - first, group)
                for dst, x, y in zip((ph, plo), split(a), split(b)):
                    dst[u, i, spot, 0:LANES] = x
                    dst[u, i, spot, LANES : 2 * LANES] = y


def product(size, k, u, ph, plo, wh, wl):
    k1, k2, k3 = (
        triple(ph[u, i][:, 0:size], plo[u, i][:, 0:size], wh[k, i], wl[k, i])
        for i in range(3)
    )
    return k1 - k3, k1 + k2


def inner_kernel(span, width, spec, size, unroll, partial, *refs):
    blocks = refs[: len(spec)]
    cs, wh, wl, out, ph, plo = refs[len(spec) :]
    first = pl.program_id(0) * unroll
    for u in range(unroll):
        load(span, width, spec, first + u, u, partial, blocks, cs, ph, plo)
    for u in range(unroll):
        k = first + u
        out[k, 0], out[k, 1] = product(size, k, u, ph, plo, wh, wl)


def halves(unroll, span):
    return [VMEM((unroll, 3, 2 * span[1], 2 * LANES), BF16)] * 2


def inner(span, partial, blocks, spec, cs, weights):
    count, _, size, _ = weights[0].shape
    unroll = UNROLL
    while count % unroll:
        unroll //= 2
    return pl.pallas_call(
        functools.partial(inner_kernel, span, cs.shape[1] // count, spec, size, unroll),
        out_shape=kept((count, 2, 2 * span[1], size)),
        grid=(count // unroll,),
        in_specs=[WHOLE] * (4 + len(blocks)),
        out_specs=WHOLE,
        scratch_shapes=halves(unroll, span),
        compiler_params=limit(12),
        name="inner",
    )(*in_vmem(partial, *blocks, cs, *weights))


def final_kernel(span, width, spec, scale, size, unroll, done, partial, *refs):
    blocks = refs[: len(spec)]
    cs, gh, gl, wh, wl, raw, ph, plo, out, sem = refs[len(spec) :]
    half = size // 2
    first = pl.program_id(0) * unroll

    def outer(u, sums):
        k = first + u
        re, im = (jnp.concatenate([done[k, i], x], axis=0) for i, x in enumerate(sums))
        k1, k2, k3 = (
            triple(gh[k, i], gl[k, i], *split(m))
            for i, m in enumerate((re, im - re, re + im))
        )
        re, im = k1 - k3, k1 + k2
        return (re * re + im * im) * scale

    def store(u, value):
        tail = value[:, LANES:size]
        tail = jnp.concatenate([tail, tail], axis=1)
        turned = pltpu.roll(value[half:, 0:LANES], 64, 1)
        low = lax.broadcasted_iota(jnp.int32, turned.shape, 1) < 64
        out[u, pl.ds(0, half, stride=3), :] = value[0:half, 0:LANES]
        out[u, pl.ds(1, half, stride=3), :] = jnp.where(low, tail[0:half], turned)
        out[u, pl.ds(2, half, stride=3), :] = jnp.where(low, turned, tail[half:])

    for u in range(unroll):
        load(span, width, spec, first + u, u, partial, blocks, cs, ph, plo)
    sums = [product(size, first + u, u, ph, plo, wh, wl) for u in range(2)]
    copies = []
    for u in range(unroll):
        if u + 2 < unroll:
            sums.append(product(size, first + u + 2, u + 2, ph, plo, wh, wl))
        store(u, outer(u, sums[u]))
        copies.append(pltpu.make_async_copy(out.at[u], raw.at[first + u], sem.at[u]))
        copies[-1].start()
    for c in copies:
        c.wait()


def final(span, done, partial, blocks, spec, cs, lefts, weights, total):
    count, _, size, _ = weights[0].shape
    tiles = size * size // LANES
    unroll = UNROLL
    while count % unroll:
        unroll //= 2
    width = cs.shape[1] // count
    result = pl.pallas_call(
        functools.partial(final_kernel, span, width, spec, 1.0 / total, size, unroll),
        out_shape=jax.ShapeDtypeStruct((count, tiles, LANES), F32),
        grid=(count // unroll,),
        in_specs=[WHOLE] * (7 + len(blocks)),
        out_specs=RAW,
        scratch_shapes=halves(unroll, span)
        + [VMEM((unroll, tiles, LANES), F32), pltpu.SemaphoreType.DMA((unroll,))],
        compiler_params=limit(24),
        name="final",
    )(*in_vmem(done, partial, *blocks, cs, *lefts, *weights))
    return result.reshape(count, 1, size * size)


def swap(x, axis, bit, n):
    return lax.ppermute(x, axis, [(i, i ^ bit) for i in range(n)])


def edges(n):
    cycle = list(range(0, n, 2)) + list(range(n - 1, 0, -2))
    even, odd = [], []
    for i in range(0, n, 2):
        a, b, c = cycle[i], cycle[i + 1], cycle[(i + 2) % n]
        even += [(a, b), (b, a)]
        odd += [(b, c), (c, b)]
    return even, odd


def chunks(lines):
    return ((0, 2 * lines // 3), (2 * lines // 3, lines // 3))


def neighbour_gather(parts, n):
    even, odd = edges(n)
    moving = [p[None] for p in parts]
    held = [np.arange(n)[:, None] for _ in parts]
    blocks, sources = [[] for _ in parts], [[] for _ in parts]
    for step in range(n // 2):
        arrived = []
        for h in range(len(parts)):
            perm = (even, odd)[(step + h) % 2]
            arrived.append(lax.ppermute(moving[h], "row", perm))
            source = np.zeros_like(held[h])
            for a, b in perm:
                source[b] = held[h][a]
            if step == 0:
                source = np.concatenate([held[h], source], axis=1)
            held[h] = source
            sources[h].append(source)
        for h in range(len(parts)):
            if step == 0:
                arrived[h] = jnp.concatenate([moving[h], arrived[h]])
            moving[h] = arrived[h]
            blocks[h].append(moving[h])
    return blocks, [np.concatenate(s, axis=1) for s in sources]


def body(
    constants,
    current_modes,
    owner_id,
    live_count,
    triplets,
    center_point,
    pair_points,
    first_vectors,
    second_vectors,
):
    n_row, n_ba = lax.axis_size("row"), lax.axis_size("ba")
    slots, width, _ = constants.shape
    size = width * n_ba
    bands = current_modes.shape[-1]
    half = size // 2
    total = slots * n_row
    modes = jnp.swapaxes(current_modes[0], 1, 2)
    payload = pack(modes, owner_id, triplets, center_point, bands, slots, total)
    bit, hop = 1, 0
    while bit < n_row:
        if bit == FIRST and n_row >= 4 * bit:
            others = []
            for i in (1, 2, 3):
                others.append(swap(payload, "row", i * bit, n_row))
            bit *= 4
            payload = payload + others[0] + others[1] + others[2]
        else:
            other = swap(payload, "row", bit, n_row)
            bit *= 2
            if bit < n_row:
                payload = payload + other
        hop += 1
    shares = (2, 1)
    pieces, base = [], 0
    for i, share in enumerate(shares):
        rows = share * width // sum(shares) if i + 1 < len(shares) else width - base
        pieces += fetch(constants, base, rows)
        base += rows
    spans = chunks(half)
    weight = (jnp.arange(slots, dtype=jnp.int32) < live_count[0]).astype(F32)
    owns = []
    for base, lines in spans:
        keep, send = contract(pieces, payload, other, bands, base, lines)
        keep = keep.reshape(bands // 2, 2, slots, lines, 2 * size)
        send = send.reshape(bands // 2, 2, slots, lines, 2 * size)
        got = swap(send, "ba", 1, n_ba)
        far = swap(keep[1] + got[1], "ba", 2, n_ba)
        own = ((keep[0] + got[0]) + far) * weight[None, :, None, None]
        owns.append(own.swapaxes(0, 1))

    weights = prep(second_vectors, size, False, spans)
    lefts = prep(first_vectors, size, True, spans)
    if slots == 1 and n_row <= 8:
        parts, places = [], []
        for own, (base, lines) in zip(owns, spans):
            for start in (0, lines // 2):
                parts.append(own[0, :, start : start + lines // 2])
                places.append((base + start, lines // 2))
        blocks, sources = neighbour_gather(parts, n_row)
        order = np.concatenate(sources, axis=1)
        ahead, behind = [], [[] for _ in spans]
        for h, (base, lines) in enumerate(places):
            slot = h * n_row
            for n, b in enumerate(blocks[h]):
                here = range(slot, slot + b.shape[0])
                entry = (b, (base, lines, tuple(here)))
                (behind[h // 2] if n == len(blocks[h]) - 1 else ahead).append(entry)
                slot += b.shape[0]
    else:
        slots_all = tuple(range(total))
        ahead, behind = [], [[] for _ in spans]
        for own, (base, lines) in zip(owns, spans):
            gathered = lax.all_gather(own, "row", axis=0, tiled=True)
            ahead.append((gathered, (base, lines, slots_all)))
        order = np.broadcast_to(np.arange(total), (n_row, total))
    order = tuple(tuple(int(x) for x in line) for line in order)
    table = angles(payload, other, pair_points, 2 * bands, order)
    partial = early(*zip(*ahead), table, pair_points.shape[0], half)
    late = [tuple(zip(*b)) if b else ((), ()) for b in behind]
    done = inner(spans[0], partial, *late[0], table, weights)
    return final(spans[1], done, partial, *late[1], table, lefts, weights, total)


def solution(mesh):
    return jax.shard_map(
        body,
        mesh=mesh,
        in_specs=(
            P("row", "ba", None),
            P("row", None, "ba", None),
            P(),
            P("row"),
            P("row", None),
            P(),
            P("row", None),
            P("row", None, None),
            P("row", None, None),
        ),
        out_specs=P("row", "ba", None),
        check_vma=False,
    )
```

```python
import functools
import math

import jax
import jax.numpy as jnp
import numpy as np
from jax import lax
from jax.experimental import pallas as pl
from jax.experimental.pallas import tpu as pltpu
from jax.sharding import PartitionSpec as P

G = 32
UNROLL = 8
FIRST = 1
FULL_TURN = 2.0 * math.pi
LANES = 128
F32 = jnp.float32
BF16 = jnp.bfloat16
VMEM = pltpu.VMEM
SMEM = pltpu.SMEM


def split(x):
    hi = x.astype(BF16)
    lo = (x - hi.astype(F32)).astype(BF16)
    return hi, lo


def dot(a, b):
    return jnp.dot(a, b, preferred_element_type=F32)


def in_vmem(*xs):
    return [pltpu.with_memory_space_constraint(x, VMEM) for x in xs]


def in_hbm(*xs):
    return [pltpu.with_memory_space_constraint(x, pltpu.HBM) for x in xs]


def kept(shape, dtype=F32):
    return VMEM(shape, dtype)


WHOLE = pl.BlockSpec(memory_space=VMEM)
SCALARS = pl.BlockSpec(memory_space=SMEM)
RAW = pl.BlockSpec(memory_space=pltpu.HBM)


def limit(mib):
    return pltpu.CompilerParams(vmem_limit_bytes=mib << 20)


def pack_kernel(bands, slots, *refs):
    owner, raw, out, (trip, center, modes, sem) = refs[0], refs[1:4], refs[4], refs[5:]
    copies = [
        pltpu.make_async_copy(src, dst, sem.at[i])
        for i, (src, dst) in enumerate(zip(raw, (trip, center, modes)))
    ]
    for c in copies:
        c.start()
    out[...] = jnp.zeros_like(out)
    for c in copies:
        c.wait()
    row, ba = lax.axis_index("row"), lax.axis_index("ba")
    mine = (owner[0] == row).astype(F32)
    width = modes.shape[-1]
    order = [j for j in range(bands) if j % 2 == 0] + [j for j in range(bands) if j % 2]
    for place, j in enumerate(order):
        for s in range(2):
            line = modes[s, pl.ds(lax.bitwise_xor(ba, j), 1), :]
            out[pl.ds(place * 2 + s, 1), 0:width] = line * mine
    lane = lax.broadcasted_iota(jnp.int32, (1, LANES), 1)
    for r in range(slots):
        shift = 0
        entry = jnp.zeros((1, LANES), jnp.int32)
        for d in range(3):
            entry = jnp.where(lane == d, trip[r, d] - trip[r, 3 + d], entry)
            shift = shift + trip[r, 3 + d] * center[d]
        entry = jnp.where(lane == 3, shift, entry)
        out[pl.ds(2 * bands + row * slots + r, 1), :] = entry.astype(F32)


def pack(modes, owner, trip, center, bands, slots, total):
    rows = 2 * bands + -(-total // 8) * 8
    return pl.pallas_call(
        functools.partial(pack_kernel, bands, slots),
        out_shape=kept((rows, LANES)),
        in_specs=[SCALARS] + [RAW] * 3,
        out_specs=WHOLE,
        scratch_shapes=[SMEM(x.shape, x.dtype) for x in (trip, center)]
        + [VMEM(modes.shape, F32), pltpu.SemaphoreType.DMA((3,))],
        compiler_params=limit(4),
        name="pack",
    )(owner, *in_hbm(trip, center, modes))


def fetch_kernel(slots, first, rows, parts, const, hi, lo, buf, sem):
    width = const.shape[2] // parts
    copies = []
    for r in range(slots):
        for i in range(parts):
            lanes = pl.ds(i * width, width)
            copies.append(
                pltpu.make_async_copy(
                    const.at[r, pl.ds(first, rows), lanes], buf.at[r, :, lanes], sem.at[r, i]
                )
            )
    for c in copies:
        c.start()
    for n, c in enumerate(copies):
        c.wait()
        r, i = n // parts, n % parts
        lanes = slice(i * width, (i + 1) * width)
        hi[r, :, lanes], lo[r, :, lanes] = split(buf[r, :, lanes])


def fetch(constants, first, rows):
    slots, _, bb = constants.shape
    parts = 6
    return pl.pallas_call(
        functools.partial(fetch_kernel, slots, first, rows, parts),
        out_shape=(kept((slots, rows, bb), BF16),) * 2,
        in_specs=[RAW],
        out_specs=[WHOLE] * 2,
        scratch_shapes=[
            VMEM((slots, rows, bb), F32),
            pltpu.SemaphoreType.DMA((slots, parts)),
        ],
        compiler_params=limit(8),
        name="fetch",
    )(*in_hbm(constants))


def contract_kernel(bands, slots, first, lines, e0, e1, *refs):
    pieces, (keep, send, turn) = refs[:-3], refs[-3:]
    his, los = pieces[0::2], pieces[1::2]
    width = sum(h.shape[1] for h in his)
    total = e0[...] + e1[...]
    eigen = total[0 : 2 * bands, 0:width]
    pairs, chunk = keep.shape[2], keep.shape[3]
    low = lax.broadcasted_iota(jnp.int32, (2 * bands, LANES), 1) < 64
    for r in range(slots):
        eh, el = split(eigen)
        left = jnp.concatenate(
            [
                jnp.concatenate([eh, eh], axis=1),
                jnp.concatenate([el, jnp.zeros_like(el)], axis=1),
            ],
            axis=0,
        )
        for base in range(0, pairs, lines):
            lanes = slice((first + base) * chunk, (first + base + lines) * chunk)
            right = jnp.concatenate(
                [h[r, :, lanes] for h in his] + [m[r, :, lanes] for m in los], axis=0
            )
            both = dot(left, right)
            res = both[0 : 2 * bands] + both[2 * bands :]
            for q in range(lines):
                j0, j1, j2 = (
                    res[:, q * chunk + j * LANES : q * chunk + (j + 1) * LANES]
                    for j in range(3)
                )
                t1 = jnp.where(low, j1, j2)
                t2 = jnp.where(low, pltpu.roll(j1, 64, 1), pltpu.roll(j2, 64, 1))
                for j, t in enumerate((j0, t1, t2)):
                    turn[base // lines, j, pl.ds(q, 2 * bands, stride=lines), :] = t
            for row in range(2 * bands):
                dst = (keep, send)[row // bands]
                for j in range(3):
                    spot = slice(j * LANES, (j + 1) * LANES)
                    dst[row % bands, r, base : base + lines, spot] = turn[
                        base // lines, j, row * lines : (row + 1) * lines, :
                    ]


def contract(pieces, e0, e1, bands, first, count):
    slots = pieces[0].shape[0]
    return pl.pallas_call(
        functools.partial(contract_kernel, bands, slots, first, 8),
        out_shape=(kept((bands, slots, count, 3 * LANES)),) * 2,
        in_specs=[WHOLE] * (2 + len(pieces)),
        out_specs=[WHOLE] * 2,
        scratch_shapes=[VMEM((count // 8, 3, 2 * bands * 8, LANES), F32)],
        compiler_params=limit(8),
        name="contract",
    )(*in_vmem(e0, e1, *pieces))


def unpack_matrix(ref, k, s, size):
    half = size // 2
    j0, j1, j2 = (ref[k, pl.ds(2 * j + s, half, stride=6), :] for j in range(3))
    lane = lax.broadcasted_iota(jnp.int32, j0.shape, 1)
    r1 = pltpu.roll(j1, 64, 1)
    r2 = pltpu.roll(j2, 64, 1)
    return (j0, j1), (jnp.where(lane < 64, r1, r2), r2)


def join(a, b, size):
    return jnp.concatenate([a, b[:, 0 : size - LANES]], axis=1)


def prep_kernel(size, turn, spans, raw, hi, lo, buf, sem, left, right):
    half = size // 2
    count = raw.shape[0]
    copies = [
        pltpu.make_async_copy(raw.at[k], buf.at[k], sem.at[k]) for k in range(count)
    ]
    for c in copies:
        c.start()
    for k in range(count):
        copies[k].wait()
        mats = []
        for s in range(2):
            even, odd = unpack_matrix(buf, k, s, size)
            if turn:
                both = join(*even, size), join(*odd, size)
                rows = [x[a : a + n] for a, n in spans for x in both]
                turned = jnp.concatenate(rows, axis=0).T
                left[...] = turned[:, 0:LANES]
                right[:, 0 : size - LANES] = turned[:, LANES:size]
                rows = [
                    join(
                        left[pl.ds(p, half, stride=2), :],
                        right[pl.ds(p, half, stride=2), :],
                        size,
                    )
                    for p in range(2)
                ]
                mats.append(jnp.concatenate(rows, axis=0))
            else:
                for p, (a, b) in enumerate((even, odd)):
                    left[pl.ds(p, half, stride=2), :] = a
                    right[pl.ds(p, half, stride=2), :] = b
                mats.append(join(left[...], right[...], size))
        re, im = mats
        three = (re + im, re, im) if turn else (re, im - re, re + im)
        for i, m in enumerate(three):
            hi[k, i], lo[k, i] = split(m)


def prep(vectors, size, turn, spans):
    count, _, bb = vectors.shape
    tiles = bb // LANES
    view = vectors.reshape(count, 2, tiles, LANES).swapaxes(1, 2)
    view = view.reshape(count, 2 * tiles, LANES)
    return pl.pallas_call(
        functools.partial(prep_kernel, size, turn, spans),
        out_shape=(kept((count, 3, size, size), BF16),) * 2,
        in_specs=[RAW],
        out_specs=[WHOLE] * 2,
        scratch_shapes=[
            VMEM(view.shape, F32),
            pltpu.SemaphoreType.DMA((count,)),
            VMEM((size, LANES), F32),
            VMEM((size, LANES), F32),
        ],
        compiler_params=limit(8),
        name="prep",
    )(*in_hbm(view))


def angle_kernel(first, order, e0, e1, points, out):
    count, width = points.shape[1], len(order[0])
    row = lax.axis_index("row")
    lines = []
    for choice in zip(*order):
        if len(set(choice)) == 1:
            slot = choice[0]
        else:
            slot = sum(jnp.where(row == i, c, 0) for i, c in enumerate(choice))
        spot = pl.ds(first + slot, 1)
        lines.append(e0[spot, :] + e1[spot, :])
    lines = jnp.concatenate(lines, axis=0)
    cell = [jnp.broadcast_to(lines[:, d : d + 1], (width, LANES)) for d in range(4)]
    for k in range(count):
        turns = -cell[3]
        for d in range(3):
            turns = turns + cell[d] * points[d : d + 1, k : k + 1].astype(F32)
        turns = lax.rem(turns.astype(jnp.int32), G)
        turns = jnp.where(turns < 0, turns + G, turns)
        angle = turns.astype(F32) * (FULL_TURN / G)
        out[0, k * width : (k + 1) * width, :] = jnp.cos(angle)
        out[1, k * width : (k + 1) * width, :] = jnp.sin(angle)


def angles(e0, e1, points, first, order):
    lines = points.shape[0] * len(order[0])
    return pl.pallas_call(
        functools.partial(angle_kernel, first, order),
        out_shape=kept((2, lines, LANES)),
        in_specs=[WHOLE] * 3,
        out_specs=WHOLE,
        compiler_params=limit(4),
        name="angles",
    )(*in_vmem(e0, e1), points.T)


def rotated(refs, spec, cs, width, k, q0, group, re, im):
    for ref, (base, lines, slots) in zip(refs, spec):
        if not base <= q0 < base + lines:
            continue
        local = pl.ds(q0 - base, group)

        def turn(t, slot):
            spot = pl.ds(k * width + slot, 1)
            c, s = cs[0, spot, :], cs[1, spot, :]
            a, b = ref[t, 0, local, :], ref[t, 1, local, :]
            c, s = (jnp.concatenate([x] * 3, axis=1) for x in (c, s))
            return a * c - b * s, a * s + b * c

        if len(slots) <= 8:
            for t, slot in enumerate(slots):
                a, b = turn(t, slot)
                re = a if re is None else re + a
                im = b if im is None else im + b
        else:
            zero = jnp.zeros((group, 3 * LANES), F32)

            def step(t, carry):
                a, b = turn(t, t)
                return carry[0] + a, carry[1] + b

            start = (zero if re is None else re, zero if im is None else im)
            re, im = lax.fori_loop(0, len(slots), step, start)
    return re, im


def early_kernel(spec, width, group, *refs):
    blocks, cs, out = refs[: len(spec)], refs[-2], refs[-1]

    def one(k, carry):
        for q0 in range(0, out.shape[2], group):
            re, im = rotated(blocks, spec, cs, width, k, q0, group, None, None)
            out[k, 0, pl.ds(q0, group), :] = re
            out[k, 1, pl.ds(q0, group), :] = im
        return carry

    lax.fori_loop(0, out.shape[0], one, 0)


def early(blocks, spec, cs, count, half):
    width = cs.shape[1] // count
    return pl.pallas_call(
        functools.partial(early_kernel, spec, width, 8),
        out_shape=kept((count, 2, half, 3 * LANES)),
        in_specs=[WHOLE] * (len(blocks) + 1),
        out_specs=WHOLE,
        compiler_params=limit(4),
        name="early",
    )(*in_vmem(*blocks, cs))


def triple(xh, xl, yh, yl):
    rows = xh.shape[0]
    both = dot(jnp.concatenate([xh, xl], axis=0), yh)
    return both[0:rows] + both[rows:] + dot(xh, yl)


def load(span, width, spec, k, u, partial, blocks, cs, ph, plo):
    first, lines = span
    group = 16
    for q0 in range(first, first + lines, group):
        re, im = partial[k, 0, pl.ds(q0, group), :], partial[k, 1, pl.ds(q0, group), :]
        re, im = rotated(blocks, spec, cs, width, k, q0, group, re, im)
        for i, m in enumerate((re + im, re, im)):
            t0, t1, t2 = (m[:, j * LANES : (j + 1) * LANES] for j in range(3))
            for base, a, b in ((0, t0, t1), (lines, t2, pltpu.roll(t1, 64, 1))):
                spot = pl.ds(base + q0 - first, group)
                for dst, x, y in zip((ph, plo), split(a), split(b)):
                    dst[u, i, spot, 0:LANES] = x
                    dst[u, i, spot, LANES : 2 * LANES] = y


def product(size, k, u, ph, plo, wh, wl):
    k1, k2, k3 = (
        triple(ph[u, i][:, 0:size], plo[u, i][:, 0:size], wh[k, i], wl[k, i])
        for i in range(3)
    )
    return k1 - k3, k1 + k2


def inner_kernel(span, width, spec, size, unroll, partial, *refs):
    blocks = refs[: len(spec)]
    cs, wh, wl, out, ph, plo = refs[len(spec) :]
    first = pl.program_id(0) * unroll
    for u in range(unroll):
        load(span, width, spec, first + u, u, partial, blocks, cs, ph, plo)
    for u in range(unroll):
        k = first + u
        out[k, 0], out[k, 1] = product(size, k, u, ph, plo, wh, wl)


def halves(unroll, span):
    return [VMEM((unroll, 3, 2 * span[1], 2 * LANES), BF16)] * 2


def inner(span, partial, blocks, spec, cs, weights):
    count, _, size, _ = weights[0].shape
    unroll = UNROLL
    while count % unroll:
        unroll //= 2
    return pl.pallas_call(
        functools.partial(inner_kernel, span, cs.shape[1] // count, spec, size, unroll),
        out_shape=kept((count, 2, 2 * span[1], size)),
        grid=(count // unroll,),
        in_specs=[WHOLE] * (4 + len(blocks)),
        out_specs=WHOLE,
        scratch_shapes=halves(unroll, span),
        compiler_params=limit(12),
        name="inner",
    )(*in_vmem(partial, *blocks, cs, *weights))


def final_kernel(span, width, spec, scale, size, unroll, done, partial, *refs):
    blocks = refs[: len(spec)]
    cs, gh, gl, wh, wl, raw, ph, plo, out, sem = refs[len(spec) :]
    half = size // 2
    first = pl.program_id(0) * unroll

    def outer(u, sums):
        k = first + u
        re, im = (jnp.concatenate([done[k, i], x], axis=0) for i, x in enumerate(sums))
        k1, k2, k3 = (
            triple(gh[k, i], gl[k, i], *split(m))
            for i, m in enumerate((re, im - re, re + im))
        )
        re, im = k1 - k3, k1 + k2
        return (re * re + im * im) * scale

    def store(u, value):
        tail = value[:, LANES:size]
        tail = jnp.concatenate([tail, tail], axis=1)
        turned = pltpu.roll(value[half:, 0:LANES], 64, 1)
        low = lax.broadcasted_iota(jnp.int32, turned.shape, 1) < 64
        out[u, pl.ds(0, half, stride=3), :] = value[0:half, 0:LANES]
        out[u, pl.ds(1, half, stride=3), :] = jnp.where(low, tail[0:half], turned)
        out[u, pl.ds(2, half, stride=3), :] = jnp.where(low, turned, tail[half:])

    for u in range(unroll):
        load(span, width, spec, first + u, u, partial, blocks, cs, ph, plo)
    sums = [product(size, first + u, u, ph, plo, wh, wl) for u in range(2)]
    copies = []
    for u in range(unroll):
        if u + 2 < unroll:
            sums.append(product(size, first + u + 2, u + 2, ph, plo, wh, wl))
        store(u, outer(u, sums[u]))
        copies.append(pltpu.make_async_copy(out.at[u], raw.at[first + u], sem.at[u]))
        copies[-1].start()
    for c in copies:
        c.wait()


def final(span, done, partial, blocks, spec, cs, lefts, weights, total):
    count, _, size, _ = weights[0].shape
    tiles = size * size // LANES
    unroll = UNROLL
    while count % unroll:
        unroll //= 2
    width = cs.shape[1] // count
    result = pl.pallas_call(
        functools.partial(final_kernel, span, width, spec, 1.0 / total, size, unroll),
        out_shape=jax.ShapeDtypeStruct((count, tiles, LANES), F32),
        grid=(count // unroll,),
        in_specs=[WHOLE] * (7 + len(blocks)),
        out_specs=RAW,
        scratch_shapes=halves(unroll, span)
        + [VMEM((unroll, tiles, LANES), F32), pltpu.SemaphoreType.DMA((unroll,))],
        compiler_params=limit(24),
        name="final",
    )(*in_vmem(done, partial, *blocks, cs, *lefts, *weights))
    return result.reshape(count, 1, size * size)


def swap(x, axis, bit, n):
    return lax.ppermute(x, axis, [(i, i ^ bit) for i in range(n)])


def edges(n):
    cycle = list(range(0, n, 2)) + list(range(n - 1, 0, -2))
    even, odd = [], []
    for i in range(0, n, 2):
        a, b, c = cycle[i], cycle[i + 1], cycle[(i + 2) % n]
        even += [(a, b), (b, a)]
        odd += [(b, c), (c, b)]
    return even, odd


def chunks(lines):
    return ((0, 2 * lines // 3), (2 * lines // 3, lines // 3))


def neighbour_gather(parts, n):
    even, odd = edges(n)
    moving = [p[None] for p in parts]
    held = [np.arange(n)[:, None] for _ in parts]
    blocks, sources = [[] for _ in parts], [[] for _ in parts]
    for step in range(n // 2):
        arrived = []
        for h in range(len(parts)):
            perm = (even, odd)[(step + h) % 2]
            arrived.append(lax.ppermute(moving[h], "row", perm))
            source = np.zeros_like(held[h])
            for a, b in perm:
                source[b] = held[h][a]
            if step == 0:
                source = np.concatenate([held[h], source], axis=1)
            held[h] = source
            sources[h].append(source)
        for h in range(len(parts)):
            if step == 0:
                arrived[h] = jnp.concatenate([moving[h], arrived[h]])
            moving[h] = arrived[h]
            blocks[h].append(moving[h])
    return blocks, [np.concatenate(s, axis=1) for s in sources]


def body(
    constants,
    current_modes,
    owner_id,
    live_count,
    triplets,
    center_point,
    pair_points,
    first_vectors,
    second_vectors,
):
    n_row, n_ba = lax.axis_size("row"), lax.axis_size("ba")
    slots, width, _ = constants.shape
    size = width * n_ba
    bands = current_modes.shape[-1]
    half = size // 2
    total = slots * n_row
    modes = jnp.swapaxes(current_modes[0], 1, 2)
    payload = pack(modes, owner_id, triplets, center_point, bands, slots, total)
    bit, hop = 1, 0
    while bit < n_row:
        if bit == FIRST and n_row >= 4 * bit:
            others = []
            for i in (1, 2, 3):
                others.append(swap(payload, "row", i * bit, n_row))
            bit *= 4
            payload = payload + others[0] + others[1] + others[2]
        else:
            other = swap(payload, "row", bit, n_row)
            bit *= 2
            if bit < n_row:
                payload = payload + other
        hop += 1
    shares = (2, 1)
    pieces, base = [], 0
    for i, share in enumerate(shares):
        rows = share * width // sum(shares) if i + 1 < len(shares) else width - base
        pieces += fetch(constants, base, rows)
        base += rows
    spans = chunks(half)
    weight = (jnp.arange(slots, dtype=jnp.int32) < live_count[0]).astype(F32)
    owns = []
    for base, lines in spans:
        keep, send = contract(pieces, payload, other, bands, base, lines)
        keep = keep.reshape(bands // 2, 2, slots, lines, 2 * size)
        send = send.reshape(bands // 2, 2, slots, lines, 2 * size)
        got = swap(send, "ba", 1, n_ba)
        far = swap(keep[1] + got[1], "ba", 2, n_ba)
        own = ((keep[0] + got[0]) + far) * weight[None, :, None, None]
        owns.append(own.swapaxes(0, 1))

    weights = prep(second_vectors, size, False, spans)
    lefts = prep(first_vectors, size, True, spans)
    if slots == 1 and n_row <= 8:
        parts, places = [], []
        for own, (base, lines) in zip(owns, spans):
            for start in (0, lines // 2):
                parts.append(own[0, :, start : start + lines // 2])
                places.append((base + start, lines // 2))
        blocks, sources = neighbour_gather(parts, n_row)
        order = np.concatenate(sources, axis=1)
        ahead, behind = [], [[] for _ in spans]
        for h, (base, lines) in enumerate(places):
            slot = h * n_row
            for n, b in enumerate(blocks[h]):
                here = range(slot, slot + b.shape[0])
                entry = (b, (base, lines, tuple(here)))
                (behind[h // 2] if n == len(blocks[h]) - 1 else ahead).append(entry)
                slot += b.shape[0]
    else:
        slots_all = tuple(range(total))
        ahead, behind = [], [[] for _ in spans]
        for own, (base, lines) in zip(owns, spans):
            gathered = lax.all_gather(own, "row", axis=0, tiled=True)
            ahead.append((gathered, (base, lines, slots_all)))
        order = np.broadcast_to(np.arange(total), (n_row, total))
    order = tuple(tuple(int(x) for x in line) for line in order)
    table = angles(payload, other, pair_points, 2 * bands, order)
    partial = early(*zip(*ahead), table, pair_points.shape[0], half)
    late = [tuple(zip(*b)) if b else ((), ()) for b in behind]
    done = inner(spans[0], partial, *late[0], table, weights)
    return final(spans[1], done, partial, *late[1], table, lefts, weights, total)


def solution(mesh):
    return jax.shard_map(
        body,
        mesh=mesh,
        in_specs=(
            P("row", "ba", None),
            P("row", None, "ba", None),
            P(),
            P("row"),
            P("row", None),
            P(),
            P("row", None),
            P("row", None, None),
            P("row", None, None),
        ),
        out_specs=P("row", "ba", None),
        check_vma=False,
    )
```
